32 devices in a mesh: cam: 2 (over y), tm: 16 (over z, x, core).
Axes of the slice: x: 2, y: 2, z: 4, core: 2. Of those that a mesh axis runs over, the one named last changes fastest.
Arguments:
- keypoints: int32 [4, 34, 8192], P('cam', None, 'tm'), may hold values from 0 to 4095
- visibility: int32 [4, 8192], P(None, 'tm'), may hold values 0 or 1
- expand_weight: bfloat16 [3, 34, 1024], replicated, may hold values from -0.625 to 0.625
- dilated_tap_weight: bfloat16 [1024, 3, 1024], P('tm'), may hold values from -0.109375 to 0.109375
- join_weight: bfloat16 [1024, 64], replicated, may hold values from -0.1875 to 0.1875
- decay_rates: float32 [64, 8192], P('cam', 'tm'), may hold values from 0 to 1, as said below
Outputs:
- smoothed: float32 [64, 8192], P('cam', 'tm')
The draws below stay inside these ranges and needn't reach their ends.
Inputs may be any that keep to these rules, and one draw needn't show every extreme that they name: `keypoints`: quantized image coordinates. `decay_rates`: positive rates.
All inputs are finite; a program needn't handle non-finite values. No bound on the sum of `visibility` on one device may be relied on, other than what follows from the above.
Results may differ from the reference program's by a relative error of at most 0.00045.
Values may be sent and summed in bfloat16 or wider, within the bound.
A program may use at most 64 MiB of HBM per device.

```python
import jax
import jax.numpy as jnp
from jax import lax

C = 1024
J2 = 34
STATE = 64
DILATION_STEP = 3
FR_DEV = 512
CAMERAS = 4
CLIP_LENGTH = 8192


def draw_decay_rates(key, part):
    keys = jax.random.split(key, 7)
    slow_flag = jax.random.randint(keys[0], (STATE, 1), 0, 2) == 1
    fast_rate = jnp.exp(jax.random.uniform(keys[1], (STATE, 1), jnp.float32, jnp.log(1.0 / 50.0), jnp.log(1.0 / 30.0)))
    slow_rate = jnp.exp(jax.random.uniform(keys[2], (STATE, 1), jnp.float32, jnp.log(0.05), jnp.log(0.4))) / CLIP_LENGTH
    reference_decay_speed = jnp.where(slow_flag, slow_rate, fast_rate)
    interval_multiplier = jnp.exp(jax.random.uniform(keys[3], (STATE, CLIP_LENGTH // FR_DEV), jnp.float32, jnp.log(0.5), jnp.log(2.0)))
    interval_multiplier = jnp.repeat(interval_multiplier, FR_DEV, axis=1)
    instant_multiplier = jnp.exp(jax.random.uniform(keys[4], (STATE, CLIP_LENGTH), jnp.float32, jnp.log(0.5), jnp.log(2.0)))
    marker_locations = jax.random.randint(keys[5], (2,), 0, CLIP_LENGTH)
    retain_flags = jax.random.uniform(keys[6], (2,), jnp.float32, 0.5, 0.8)
    moment_number = jnp.arange(CLIP_LENGTH)
    spike_trace = jnp.zeros((CLIP_LENGTH,), jnp.float32)
    for chosen_location in range(2):
        spike_trace = spike_trace + jnp.where(moment_number == marker_locations[chosen_location], -jnp.log(retain_flags[chosen_location]), 0.0)
    return (reference_decay_speed * interval_multiplier * instant_multiplier + spike_trace[None, :]).astype(jnp.float32)


def place_ends(result, stream_key, low, high):
    index_at = [jax.random.randint(jax.random.fold_in(stream_key, axis), (), 0, length) for axis, length in enumerate(result.shape)]
    longest = result.shape.index(max(result.shape))
    next_to = index_at[:longest] + [(index_at[longest] + 1) % result.shape[longest]] + index_at[longest + 1:]
    return result.at[tuple(index_at)].set(low).at[tuple(next_to)].set(high)


def shard_levels(own_key, extent, cuts, low, top_value):
    loudness, own = 1.0, jax.random.fold_in(own_key, 6)
    for position, blocks in cuts:
        heights = jnp.exp(jax.random.uniform(jax.random.fold_in(own, position), (blocks,), jnp.float32, low / len(cuts), top_value / len(cuts)))
        loudness = loudness * jnp.repeat(heights, extent[position] // blocks).reshape([-1 if axis == position else 1 for axis in range(len(extent))])
    return loudness


def normal_values(rng, extent, deviation, most, pieces=(), dtype=jnp.bfloat16):
    result = deviation * jax.random.normal(rng, extent, jnp.float32)
    if pieces:
        result = result * shard_levels(rng, extent, pieces, -0.22, 0.18)
    return jnp.clip(result, -most, most).astype(dtype)


def setup_inputs(seed: int = 0) -> dict:
    key_list = jax.random.split(jax.random.key(seed), 7)
    keypoints = place_ends(jax.random.randint(key_list[0], (CAMERAS, J2, CLIP_LENGTH), 0, 4096), jax.random.fold_in(key_list[0], 1), 0, 4095).astype(jnp.int32)
    visibility = place_ends((jax.random.randint(key_list[1], (CAMERAS, CLIP_LENGTH), 0, 4) < 1).astype(jnp.int32), jax.random.fold_in(key_list[1], 1), 0, 1)
    expand_weight = normal_values(key_list[2], (3, J2, C), (3 * J2) ** -0.5, 0.625)
    dilated_tap_weight = normal_values(key_list[3], (C, 3, C), (3 * C) ** -0.5, 0.109375, ((0, 16),))
    join_weight = normal_values(key_list[4], (C, STATE), C ** -0.5, 0.1875)
    decay_rates = draw_decay_rates(jax.random.fold_in(key_list[6], 71), 0)
    return dict(keypoints=keypoints, visibility=visibility, expand_weight=expand_weight, dilated_tap_weight=dilated_tap_weight, join_weight=join_weight, decay_rates=decay_rates)


def reference(keypoints, visibility, expand_weight, dilated_tap_weight, join_weight, decay_rates):
    count_of_frames = keypoints.shape[2]

    def one_view(inputs):
        codes, seen_row = inputs
        coords = ((codes.astype(jnp.float32) - 2048.0) / 2048.0).astype(jnp.bfloat16)
        padded_input = jnp.pad(coords, ((0, 0), (1, 1)))
        first = jnp.zeros((count_of_frames, C), jnp.float32)
        for shift_amount in range(3):
            first = first + jnp.dot(padded_input[:, shift_amount:shift_amount + count_of_frames].T, expand_weight[shift_amount], preferred_element_type=jnp.float32)
        hidden_start0 = jax.nn.relu(first).astype(jnp.bfloat16)
        widened_output = jnp.pad(hidden_start0, ((DILATION_STEP, DILATION_STEP), (0, 0)))
        mixed_features = jnp.zeros((count_of_frames, C), jnp.float32)
        for shift_amount in range(3):
            mixed_features = mixed_features + jnp.dot(widened_output[shift_amount * DILATION_STEP:shift_amount * DILATION_STEP + count_of_frames], dilated_tap_weight[:, shift_amount, :].T, preferred_element_type=jnp.float32)
        hidden1 = (hidden_start0.astype(jnp.float32) + jax.nn.relu(mixed_features)).astype(jnp.bfloat16)
        projected = jnp.dot(hidden1, join_weight, preferred_element_type=jnp.float32)
        return (projected * seen_row.astype(jnp.float32)[:, None]).T
    terms = lax.map(one_view, (keypoints, visibility))
    total = lax.optimization_barrier(jnp.sum(terms, axis=0))
    seen = lax.optimization_barrier(jnp.sum(visibility.astype(jnp.float32), axis=0))
    joined = total / jnp.maximum(seen, 1.0)[None, :]
    decay = jnp.exp(-decay_rates)
    energy = -jnp.expm1(-2.0 * decay_rates)
    drive = jnp.sqrt(energy)

    def forward_step(state, inputs):
        factor, gain, value = inputs
        state = factor * state + gain * value
        return (state, state)
    start = jnp.zeros((decay_rates.shape[0],), jnp.float32)
    _, filtered = lax.scan(forward_step, start, (decay.T, drive.T, joined.T))

    def backward_step(state, inputs):
        factor, weight, value = inputs
        state = factor * state + weight * value
        return (state, state)
    _, smoothed = lax.scan(backward_step, start, (decay.T, energy.T, filtered), reverse=True)
    return smoothed.T
```

```python
import functools

import jax
import jax.numpy as jnp
from jax import lax
from jax.experimental import pallas as pl
from jax.experimental.pallas import tpu as pltpu
from jax.sharding import PartitionSpec as P

DILATION_STEP = 3
MESH = pl.DeviceIdType.MESH


def with_halo(array, sides, width):
    for axis, dim in sides:
        count, length = (lax.axis_size(axis), array.shape[dim])
        up = [(i, (i + 1) % count) for i in range(count - 1)]
        down = [(j, i) for i, j in up]
        last = lax.slice_in_dim(array, length - width, length, axis=dim)
        initial = lax.slice_in_dim(array, 0, width, axis=dim)
        before = lax.ppermute(last, axis, up)
        after = lax.ppermute(initial, axis, down)
        array = jnp.concatenate([before, array, after], axis=dim)
    return array


def entering(part, axis, combine, identity, reverse):
    count = lax.axis_size(axis)
    place = lax.axis_index(axis)
    ahead = count - 1 - place if reverse else place
    gathered = jax.tree.map(lambda a: lax.all_gather(a, axis), part)
    state = jax.tree.map(lambda a, e: jnp.zeros_like(a) + jnp.asarray(e, a.dtype), part, identity)

    def one(turn, state):
        source = count - 1 - turn if reverse else turn
        return combine(
            state, jax.tree.map(lambda a: lax.dynamic_index_in_dim(a, source, 0, False), gathered)
        )

    return lax.fori_loop(0, ahead, one, state)


def expand(widened_output, expand_weight, width):
    total = None
    for shift_amount in range(3):
        term = jnp.einsum(
            "vjt,jc->vtc",
            widened_output[:, :, shift_amount : shift_amount + width],
            expand_weight[shift_amount],
            preferred_element_type=jnp.float32,
        )
        total = term if total is None else total + term
    return jax.nn.relu(total).astype(jnp.bfloat16)


def dilate(padded_input, hidden_start0, weight_rows):
    count_of_frames = hidden_start0.shape[1]
    total = None
    for shift_amount in range(3):
        term = jnp.einsum(
            "vti,ni->vtn",
            padded_input[
                :, shift_amount * DILATION_STEP : shift_amount * DILATION_STEP + count_of_frames
            ],
            weight_rows[:, shift_amount],
            preferred_element_type=jnp.float32,
        )
        total = term if total is None else total + term
    residual = hidden_start0.astype(jnp.float32)
    return (residual + jax.nn.relu(total)).astype(jnp.bfloat16)


def chain(earlier, latter):
    return (earlier[0] * latter[0], latter[0] * earlier[1] + latter[1])


def body(keypoints, visibility, expand_weight, dilated_tap_weight, join_weight, decay_rates):
    view_count = keypoints.shape[0]
    count_of_frames = keypoints.shape[2]
    coords = ((keypoints.astype(jnp.float32) - 2048.0) / 2048.0).astype(jnp.bfloat16)
    widened_output = with_halo(coords, (("tm", 2),), 1)
    hidden_start0 = expand(widened_output, expand_weight, count_of_frames)
    padded_input = with_halo(hidden_start0, (("tm", 1),), DILATION_STEP)
    hidden1 = dilate(
        padded_input, hidden_start0, lax.all_gather(dilated_tap_weight, "tm", axis=0, tiled=True)
    )
    own_mask = lax.dynamic_slice_in_dim(
        visibility, lax.axis_index("cam") * view_count, view_count, 0
    )
    masked = hidden1 * own_mask[:, :, None].astype(jnp.bfloat16)
    state_rows = decay_rates.shape[0]
    total = lax.psum_scatter(
        jnp.einsum("vti,is->st", masked, join_weight, preferred_element_type=jnp.float32).astype(
            jnp.bfloat16
        ),
        "cam",
        scatter_dimension=0,
        tiled=True,
    ).astype(jnp.float32)
    seen = jnp.sum(visibility.astype(jnp.float32), axis=0)
    joined = total / jnp.maximum(seen, 1.0)[None, :]
    decay = jnp.exp(-decay_rates)
    energy = -jnp.expm1(-2.0 * decay_rates)
    drive = jnp.sqrt(energy)
    prod_fwd, local_fwd = lax.associative_scan(chain, (decay, drive * joined), axis=1)
    ones_vec = jnp.ones((state_rows,), jnp.float32)
    zeros_vec = jnp.zeros((state_rows,), jnp.float32)
    carried = entering(
        (prod_fwd[:, -1], local_fwd[:, -1]), "tm", chain, (ones_vec, zeros_vec), False
    )
    filtered = local_fwd + prod_fwd * carried[1][:, None]
    prod_back, local_back = lax.associative_scan(
        chain, (decay, energy * filtered), axis=1, reverse=True
    )
    returned = entering(
        (prod_back[:, 0], local_back[:, 0]), "tm", chain, (ones_vec, zeros_vec), True
    )
    smoothed = local_back + prod_back * returned[1][:, None]
    return smoothed

LANES = 128
DEPTH = 72
EDGE = 4
SLOT = 8


def neg_expm1(u):
    series = jnp.ones_like(u)
    for k in range(11, 1, -1):
        series = 1.0 - series * u * (1.0 / k)
    return jnp.where(u < 0.5, u * series, 1.0 - jnp.exp(-u))


def block_kernel(
    layers, keys_ref, vis_ref, raw_ref, taps_ref, join_ref, rates_ref, out_ref,
    stage, coords, edge_in, first_wide, first, weights, hidden, slab_in, slab_hidden, slab_mixed,
    mixed, masks, joiner, powers, kept_forms, part_out, part_in, ends,
    edge_send, edge_recv, body_up, body_down, body_recv, halo_up, halo_down, halo_recv,
    mate_send, mate_recv, x_send, x_recv, y_send, y_recv, pass_send, pass_recv,
    part_send, part_recv, end_send, end_recv,
):
    joints, views, length = keys_ref.shape
    channels = raw_ref.shape[2]
    rows = taps_ref.shape[1]
    states = rates_ref.shape[0]
    cams = 2
    group = 4
    count = layers * group
    halfrows = rows // 2
    pair = 2 * rows
    wide = length + LANES
    f32, bf16 = jnp.float32, jnp.bfloat16
    y = lax.axis_index("cam")
    i = lax.axis_index("tm")
    z = i // group
    l = i % group
    x = l // 2
    c = l % 2
    mate = z * group + 2 * x + 1 - c
    across = z * group + 2 * (1 - x) + c
    outer = jnp.where(c == 0, i - 1, i + 1)
    has_outer = (outer >= 0) & (outer < count)

    barrier = pltpu.get_barrier_semaphore()

    def greet(cam, tm):
        pl.semaphore_signal(barrier, inc=1, device_id=(cam, tm), device_id_type=MESH)

    greet(y, mate)
    greet(y, across)
    greet(1 - y, i)

    @pl.when(z > 0)
    def _():
        greet(y, i - group)

    @pl.when(z < layers - 1)
    def _():
        greet(y, i + group)

    @pl.when(has_outer)
    def _():
        greet(y, outer)

    stage[...] = jnp.zeros_like(stage)
    for v in range(views):
        stage[pl.ds(v * joints, joints), :] = (keys_ref[:, v, :].astype(f32) - 2048.0) / 2048.0
        stage[pl.ds(views * joints + v, 1), :] = vis_ref[pl.ds(y * views + v, 1), :].astype(f32)
    coords[z, :, 0:length] = stage[...].astype(bf16)

    @pl.when(i == 0)
    def _():
        edge_in[0] = jnp.zeros((DEPTH, LANES), bf16)

    @pl.when(i == count - 1)
    def _():
        edge_in[1] = jnp.zeros((DEPTH, LANES), bf16)

    extra = jnp.where(z > 0, 1, 0) + jnp.where(z < layers - 1, 1, 0) + jnp.where(has_outer, 1, 0)
    pl.semaphore_wait(barrier, 3 + extra)

    def remote(src, dst, send_sem, recv_sem, cam, tm):
        return pltpu.make_async_remote_copy(
            src_ref=src, dst_ref=dst, send_sem=send_sem, recv_sem=recv_sem,
            device_id=(cam, tm), device_id_type=MESH,
        )

    def edge_copy(to_mate):
        last = (c == 0) if to_mate else (c == 1)
        lanes = pl.ds(pl.multiple_of(jnp.where(last, length - LANES, 0), LANES), LANES)
        at = c if to_mate else 1 - c
        return remote(
            coords.at[z, :, lanes], edge_in.at[at], edge_send.at[0 if to_mate else 1],
            edge_recv.at[at], y, mate if to_mate else outer,
        )

    def line_copy(source, target, halo, upward):
        at = coords.at[source, :, pl.ds(length, LANES) if halo else pl.ds(0, length)]
        if halo:
            send, recv = (halo_up if upward else halo_down), halo_recv
        else:
            send, recv = (body_up if upward else body_down), body_recv
        return remote(at, at, send.at[source], recv.at[source], y, target * group + l)

    def pass_on(source, halo, upward):
        if upward:
            @pl.when(z < layers - 1)
            def _():
                line_copy(source, z + 1, halo, True).start()
        else:
            @pl.when(z > 0)
            def _():
                line_copy(source, z - 1, halo, False).start()

    def arrive(hop):
        for halo in (False, True):
            @pl.when(z >= hop)
            def _():
                line_copy(z - hop, z, halo, True).wait_recv()
                if hop < layers - 1:
                    pass_on(z - hop, halo, True)

            @pl.when(z + hop < layers)
            def _():
                line_copy(z + hop, z, halo, False).wait_recv()
                if hop < layers - 1:
                    pass_on(z + hop, halo, False)

    def block(xs, cs, ys, o):
        start = pl.multiple_of(cs * rows + ys * halfrows, halfrows)
        return weights.at[xs, o, pl.ds(start, halfrows), :]

    def mate_copy(o):
        dst = weights.at[x, o, pl.ds(pl.multiple_of(c * rows, rows), rows), :]
        return remote(taps_ref.at[o], dst, mate_send.at[o], mate_recv.at[o], y, mate)

    def mate_arrival(o):
        dst = weights.at[x, o, pl.ds(pl.multiple_of((1 - c) * rows, rows), rows), :]
        return remote(dst, dst, mate_send.at[o], mate_recv.at[o], y, mate)

    def x_copy(o):
        src = taps_ref.at[o, pl.ds(pl.multiple_of(y * halfrows, halfrows), halfrows), :]
        return remote(src, block(x, c, y, o), x_send.at[o], x_recv.at[o], y, across)

    def x_arrival(o):
        at = block(1 - x, c, y, o)
        return remote(at, at, x_send.at[o], x_recv.at[o], y, across)

    def y_copy(o, ys):
        at = block(1 - x, c, ys, o)
        return remote(at, at, y_send.at[o], y_recv.at[o], 1 - y, i)

    def pass_copy(o, cs, other):
        at = block(1 - x, cs, 1 - y if other else y, o)
        n = o + (3 if other else 0)
        return remote(at, at, pass_send.at[n], pass_recv.at[n], y, mate)

    edge_copy(True).start()

    @pl.when(has_outer)
    def _():
        edge_copy(False).start()

    x_copy(0).start()
    pass_on(z, False, True)
    pass_on(z, False, False)
    x_copy(1).start()
    x_copy(2).start()
    for o in range(3):
        mate_copy(o).start()

    def serve_x(o):
        x_arrival(o).wait_recv()
        y_copy(o, y).start()
        pass_copy(o, c, False).start()

    def serve_y(o):
        y_copy(o, 1 - y).wait_recv()
        pass_copy(o, c, True).start()

    first_wide[...] = jnp.zeros_like(first_wide)
    for o in range(3):
        first_wide[pl.ds(o * DEPTH, joints), :] = raw_ref[o].astype(f32)
    turned = first_wide[...].T
    first[0] = turned[:, : 3 * DEPTH].astype(bf16)
    first[1] = pltpu.roll(turned, joints, 1)[:, : 3 * DEPTH].astype(bf16)
    weights[x, :, pl.ds(pl.multiple_of(c * rows, rows), rows), :] = taps_ref[...]
    for n, xs in ((0, x), (1, 1 - x)):
        joiner[:, n * pair : (n + 1) * pair] = join_ref[
            :, pl.ds(pl.multiple_of(z * 2 * pair + xs * pair, pair), pair)
        ]

    remote(edge_in.at[1 - c], edge_in.at[1 - c], edge_send.at[0], edge_recv.at[1 - c], y, mate).wait_recv()

    @pl.when(has_outer)
    def _():
        remote(edge_in.at[c], edge_in.at[c], edge_send.at[1], edge_recv.at[c], y, outer).wait_recv()

    slab_lane = lax.broadcasted_iota(jnp.int32, (DEPTH, LANES), 1)
    coords[z, :, length:wide] = jnp.where(
        slab_lane < EDGE,
        edge_in[1].astype(f32),
        jnp.where(slab_lane >= LANES - EDGE, edge_in[0].astype(f32), 0.0),
    ).astype(bf16)
    pass_on(z, True, True)
    pass_on(z, True, False)

    def source(k):
        if k == 0:
            return z
        if k == 1:
            return jnp.where(z < layers - 1, z + 1, z - 1)
        if k == 2:
            return jnp.where(z == 0, 2, z - 1 - jnp.where(z == layers - 1, 1, 0))
        return jnp.where(z < 2, 3, 0)

    sources = [source(k) for k in range(layers)]
    edge_lane = lax.broadcasted_iota(jnp.int32, (3 * DEPTH, LANES), 1)
    slab_in[...] = jnp.zeros_like(slab_in)

    def expand_shard(k):
        s = sources[k]
        e = coords[s].astype(f32)
        xs = jnp.concatenate([pltpu.roll(e, 1, 1), e, pltpu.roll(e, wide - 1, 1)], axis=0)
        masks[k] = e[DEPTH - 8 : DEPTH, 0:length]
        shard = s * group + l
        keep = ((edge_lane < DILATION_STEP) & (shard < count - 1)) | (
            (edge_lane >= LANES - DILATION_STEP) & (shard > 0)
        )
        tile = jnp.where(keep, xs[:, length:wide], 0.0)
        if k > 0:
            tile = pltpu.roll(tile, SLOT * k, 1)
        slab_in[...] += tile
        body = xs[:, 0:length].astype(bf16)
        for v in range(views):
            h = jnp.dot(first[v], body, preferred_element_type=f32)
            hidden[k, v] = jnp.maximum(h, 0.0).astype(bf16)

    own_rows = weights.at[x]
    other_rows = weights.at[1 - x]

    def early(k):
        w = own_rows[...].reshape(3 * pair, channels)
        for v in range(views):
            mixed[k, v] = jnp.dot(w, hidden[k, v], preferred_element_type=f32)

    serve_x(0)
    expand_shard(0)
    arrive(1)
    serve_x(1)
    expand_shard(1)
    serve_x(2)
    serve_y(0)
    for o in range(3):
        mate_arrival(o).wait_recv()
    early(0)
    arrive(2)
    serve_y(1)
    expand_shard(2)
    early(1)
    serve_y(2)
    arrive(3)
    expand_shard(3)
    early(2)
    early(3)

    tile = slab_in[...].astype(bf16)
    for v in range(views):
        h = jnp.dot(first[v], tile, preferred_element_type=f32)
        slab_hidden[:, v * LANES : (v + 1) * LANES] = jnp.maximum(h, 0.0).astype(bf16)
    slab_mixed[0] = jnp.dot(
        own_rows[...].reshape(3 * pair, channels), slab_hidden[...], preferred_element_type=f32
    )
    for n in range(2):
        for o in range(3):
            pass_copy(o, 1 - c, bool(n)).wait_recv()
    slab_mixed[1] = jnp.dot(
        other_rows[...].reshape(3 * pair, channels), slab_hidden[...], preferred_element_type=f32
    )

    lane = lax.broadcasted_iota(jnp.int32, (states, length), 1)

    bits = length.bit_length() - 1

    def place(step, reverse):
        turn = length - step if reverse else step
        return turn, (lane < length - step) if reverse else (lane >= step)

    def products(prod, reverse):
        for k in range(bits):
            powers[int(reverse) * bits + k] = prod
            turn, fits = place(1 << k, reverse)
            prod = prod * jnp.where(fits, pltpu.roll(prod, turn, 1), 1.0)
        return prod

    def scan(value, reverse):
        for k in range(bits):
            turn, fits = place(1 << k, reverse)
            moved = jnp.where(fits, pltpu.roll(value, turn, 1), 0.0)
            value = value + powers[int(reverse) * bits + k] * moved
        return value

    rates = rates_ref[...]
    decay = jnp.exp(-rates)
    energy = neg_expm1(2.0 * rates)
    kept_forms[0] = products(decay, False)
    kept_forms[1] = products(decay, True)
    kept_forms[2] = scan(energy * kept_forms[0], True)
    kept_forms[3] = energy
    kept_forms[4] = jnp.sqrt(energy)

    def part_copy(k, cam, tm):
        return remote(
            part_out.at[k, cam], part_in.at[z * cams + y], part_send.at[k * cams + cam],
            part_recv.at[z * cams + y], cam, tm,
        )

    def lift(a, n, k, v, rest):
        side = slab_mixed[n, :, v * LANES : (v + 1) * LANES]
        if k > 0:
            side = pltpu.roll(side, LANES - SLOT * k, 1)
        left = pltpu.roll(
            jnp.concatenate([a[0:pair], side[0:pair]], axis=1), DILATION_STEP, 1
        )[:, :length]
        right = pltpu.roll(
            jnp.concatenate([a[2 * pair :], side[2 * pair :]], axis=1), wide - DILATION_STEP, 1
        )[:, :length]
        acc = left + a[pair : 2 * pair] + right
        return (rest.astype(f32) + jnp.maximum(acc, 0.0)).astype(bf16)

    def own_channels(k, v, xs):
        return hidden[k, v, pl.ds(pl.multiple_of(z * 2 * pair + xs * pair, pair), pair), :]

    for k in range(layers - 1, -1, -1):
        total = jnp.zeros((cams * states, length), f32)
        for v in range(views):
            b = jnp.dot(
                other_rows[...].reshape(3 * pair, channels), hidden[k, v], preferred_element_type=f32
            )
            h = jnp.concatenate(
                [
                    lift(mixed[k, v], 0, k, v, own_channels(k, v, x)),
                    lift(b, 1, k, v, own_channels(k, v, 1 - x)),
                ],
                axis=0,
            )
            at = views * joints % 8 + v
            total = total + masks[k, at : at + 1, :] * jnp.dot(
                joiner[...], h, preferred_element_type=f32
            )
        for cam in range(cams):
            part_out[k, cam] = total[cam * states : (cam + 1) * states].astype(bf16)
        if k > 0:
            for cam in range(cams):
                part_copy(k, cam, sources[k] * group + l).start()
        else:
            part_copy(0, 1 - y, i).start()
            part_in[z * cams + y] = part_out[0, y]

    seen = jnp.sum(vis_ref[...].astype(f32), axis=0, keepdims=True)
    members = cams * layers
    me = z * cams + y
    for d in range(1, members):
        other = lax.rem(me + d, members)
        remote(
            part_in.at[other], part_in.at[other], part_send.at[0], part_recv.at[other],
            other % cams, (other // cams) * group + l,
        ).wait_recv()
    summed = part_in[0].astype(f32)
    for p in range(1, members):
        summed = summed + part_in[p].astype(f32)
    joined = summed / jnp.maximum(seen, 1.0)

    local = scan(kept_forms[4] * joined, False)
    back = scan(kept_forms[3] * local, True)
    prod_fwd, prod_back, through = kept_forms[0], kept_forms[1], kept_forms[2]

    square = lax.broadcasted_iota(jnp.int32, (states, LANES), 1)
    packed = jnp.where(
        square == 0,
        prod_fwd[:, length - 1 : length],
        jnp.where(
            square == 1,
            local[:, length - 1 : length],
            jnp.where(square == 2, back[:, 0:1], through[:, 0:1]),
        ),
    )
    packed = jnp.concatenate([packed, jnp.zeros((LANES - states, LANES), f32)], axis=0)
    ends[i] = packed.T[0:8]

    def end_copy(origin, target, sem):
        return remote(ends.at[origin], ends.at[origin], sem, end_recv.at[origin], y, target)

    for d in range(1, count):
        target = lax.rem(i + d, count)
        end_copy(i, target, end_send.at[target]).start()
    for d in range(1, count):
        origin = lax.rem(i + count - d, count)
        end_copy(origin, origin, end_send.at[origin]).wait_recv()

    entry = jnp.zeros((1, LANES), f32)
    carried = entry
    entries = []
    for j in range(count):
        entries.append(entry)
        carried = jnp.where(j == i, entry, carried)
        entry = ends[j, 0:1] * entry + ends[j, 1:2]
    state = jnp.zeros((1, LANES), f32)
    returned = state
    for j in range(count - 1, -1, -1):
        returned = jnp.where(j == i, state, returned)
        state = ends[j, 0:1] * state + ends[j, 2:3] + ends[j, 3:4] * entries[j]
    both = jnp.concatenate([carried, returned, jnp.zeros((LANES - 2, LANES), f32)], axis=0).T
    out_ref[...] = back + through * both[0:states, 0:1] + prod_back * both[0:states, 1:2]

    edge_copy(True).wait_send()

    @pl.when(has_outer)
    def _():
        edge_copy(False).wait_send()

    for o in range(3):
        mate_copy(o).wait_send()
        x_copy(o).wait_send()
        y_copy(o, y).wait_send()
        pass_copy(o, c, False).wait_send()
        pass_copy(o, c, True).wait_send()
    for halo in (False, True):
        for hop in range(layers - 1):
            @pl.when((z < layers - 1) & (z - hop >= 0))
            def _():
                line_copy(z - hop, z + 1, halo, True).wait_send()

            @pl.when((z > 0) & (z + hop < layers))
            def _():
                line_copy(z + hop, z - 1, halo, False).wait_send()

    for k in range(1, layers):
        for cam in range(cams):
            part_copy(k, cam, sources[k] * group + l).wait_send()
    part_copy(0, 1 - y, i).wait_send()
    for d in range(1, count):
        target = lax.rem(i + d, count)
        end_copy(i, target, end_send.at[target]).wait_send()


def block_body(cams, count, group):
    layers = count // group

    def run(keypoints, visibility, expand_weight, dilated_tap_weight, join_weight, decay_rates):
        views, joints, length = keypoints.shape
        channels = expand_weight.shape[2]
        rows = dilated_tap_weight.shape[0]
        states = decay_rates.shape[0]
        keys = jnp.transpose(keypoints, (1, 0, 2))
        taps = jnp.transpose(dilated_tap_weight, (1, 0, 2))
        wide = length + LANES
        bits = length.bit_length() - 1
        dma, vmem = (pltpu.SemaphoreType.DMA, pltpu.VMEM)
        f32, bf16 = jnp.float32, jnp.bfloat16
        sems = [2, 2] + [layers] * 6 + [3] * 6 + [6, 6] + [cams * layers] * 2 + [count] * 2
        return pl.pallas_call(
            functools.partial(block_kernel, layers),
            out_shape=jax.ShapeDtypeStruct(decay_rates.shape, f32),
            in_specs=[pl.BlockSpec(memory_space=pltpu.VMEM)] * 6,
            out_specs=pl.BlockSpec(memory_space=pltpu.VMEM),
            scratch_shapes=[
                vmem((DEPTH, length), f32),
                vmem((layers, DEPTH, wide), bf16),
                vmem((2, DEPTH, LANES), bf16),
                vmem((2 * LANES, channels), f32),
                vmem((views, channels, 3 * DEPTH), bf16),
                vmem((2, 3, 2 * rows, channels), bf16),
                vmem((layers, views, channels, length), bf16),
                vmem((3 * DEPTH, LANES), f32),
                vmem((channels, views * LANES), bf16),
                vmem((2, 6 * rows, views * LANES), f32),
                vmem((layers, views, 6 * rows, length), f32),
                vmem((layers, 8, length), f32),
                vmem((cams * states, 4 * rows), bf16),
                vmem((2 * bits, states, length), f32),
                vmem((5, states, length), f32),
                vmem((layers, cams, states, length), bf16),
                vmem((cams * layers, states, length), bf16),
                vmem((count, 8, LANES), f32),
            ]
            + [dma((n,)) for n in sems],
            compiler_params=pltpu.CompilerParams(
                collective_id=0, has_side_effects=True, vmem_limit_bytes=58 * 1024 * 1024
            ),
        )(keys, visibility, expand_weight, taps, join_weight.T, decay_rates)

    return run


def solution(mesh):
    cams, count = mesh.shape["cam"], mesh.shape["tm"]
    group = 4
    fits = count % group == 0 and cams == 2 and count == 4 * group
    return jax.shard_map(
        block_body(cams, count, group) if fits else body,
        mesh=mesh,
        in_specs=(
            P("cam", None, "tm"),
            P(None, "tm"),
            P(),
            P("tm", None, None),
            P(),
            P("cam", "tm"),
        ),
        out_specs=P("cam", "tm"),
        check_vma=False,
    )
```

```python
import functools

import jax
import jax.numpy as jnp
from jax import lax
from jax.experimental import pallas as pl
from jax.experimental.pallas import tpu as pltpu
from jax.sharding import PartitionSpec as P

DILATION_STEP = 3
MESH = pl.DeviceIdType.MESH


def with_halo(array, sides, width):
    for axis, dim in sides:
        count, length = (lax.axis_size(axis), array.shape[dim])
        up = [(i, (i + 1) % count) for i in range(count - 1)]
        down = [(j, i) for i, j in up]
        last = lax.slice_in_dim(array, length - width, length, axis=dim)
        initial = lax.slice_in_dim(array, 0, width, axis=dim)
        before = lax.ppermute(last, axis, up)
        after = lax.ppermute(initial, axis, down)
        array = jnp.concatenate([before, array, after], axis=dim)
    return array


def entering(part, axis, combine, identity, reverse):
    count = lax.axis_size(axis)
    place = lax.axis_index(axis)
    ahead = count - 1 - place if reverse else place
    gathered = jax.tree.map(lambda a: lax.all_gather(a, axis), part)
    state = jax.tree.map(lambda a, e: jnp.zeros_like(a) + jnp.asarray(e, a.dtype), part, identity)

    def one(turn, state):
        source = count - 1 - turn if reverse else turn
        return combine(
            state, jax.tree.map(lambda a: lax.dynamic_index_in_dim(a, source, 0, False), gathered)
        )

    return lax.fori_loop(0, ahead, one, state)


def expand(widened_output, expand_weight, width):
    total = None
    for shift_amount in range(3):
        term = jnp.einsum(
            "vjt,jc->vtc",
            widened_output[:, :, shift_amount : shift_amount + width],
            expand_weight[shift_amount],
            preferred_element_type=jnp.float32,
        )
        total = term if total is None else total + term
    return jax.nn.relu(total).astype(jnp.bfloat16)


def dilate(padded_input, hidden_start0, weight_rows):
    count_of_frames = hidden_start0.shape[1]
    total = None
    for shift_amount in range(3):
        term = jnp.einsum(
            "vti,ni->vtn",
            padded_input[
                :, shift_amount * DILATION_STEP : shift_amount * DILATION_STEP + count_of_frames
            ],
            weight_rows[:, shift_amount],
            preferred_element_type=jnp.float32,
        )
        total = term if total is None else total + term
    residual = hidden_start0.astype(jnp.float32)
    return (residual + jax.nn.relu(total)).astype(jnp.bfloat16)


def chain(earlier, latter):
    return (earlier[0] * latter[0], latter[0] * earlier[1] + latter[1])


def body(keypoints, visibility, expand_weight, dilated_tap_weight, join_weight, decay_rates):
    view_count = keypoints.shape[0]
    count_of_frames = keypoints.shape[2]
    coords = ((keypoints.astype(jnp.float32) - 2048.0) / 2048.0).astype(jnp.bfloat16)
    widened_output = with_halo(coords, (("tm", 2),), 1)
    hidden_start0 = expand(widened_output, expand_weight, count_of_frames)
    padded_input = with_halo(hidden_start0, (("tm", 1),), DILATION_STEP)
    hidden1 = dilate(
        padded_input, hidden_start0, lax.all_gather(dilated_tap_weight, "tm", axis=0, tiled=True)
    )
    own_mask = lax.dynamic_slice_in_dim(
        visibility, lax.axis_index("cam") * view_count, view_count, 0
    )
    masked = hidden1 * own_mask[:, :, None].astype(jnp.bfloat16)
    state_rows = decay_rates.shape[0]
    total = lax.psum_scatter(
        jnp.einsum("vti,is->st", masked, join_weight, preferred_element_type=jnp.float32).astype(
            jnp.bfloat16
        ),
        "cam",
        scatter_dimension=0,
        tiled=True,
    ).astype(jnp.float32)
    seen = jnp.sum(visibility.astype(jnp.float32), axis=0)
    joined = total / jnp.maximum(seen, 1.0)[None, :]
    decay = jnp.exp(-decay_rates)
    energy = -jnp.expm1(-2.0 * decay_rates)
    drive = jnp.sqrt(energy)
    prod_fwd, local_fwd = lax.associative_scan(chain, (decay, drive * joined), axis=1)
    ones_vec = jnp.ones((state_rows,), jnp.float32)
    zeros_vec = jnp.zeros((state_rows,), jnp.float32)
    carried = entering(
        (prod_fwd[:, -1], local_fwd[:, -1]), "tm", chain, (ones_vec, zeros_vec), False
    )
    filtered = local_fwd + prod_fwd * carried[1][:, None]
    prod_back, local_back = lax.associative_scan(
        chain, (decay, energy * filtered), axis=1, reverse=True
    )
    returned = entering(
        (prod_back[:, 0], local_back[:, 0]), "tm", chain, (ones_vec, zeros_vec), True
    )
    smoothed = local_back + prod_back * returned[1][:, None]
    return smoothed

LANES = 128
DEPTH = 72
SLOT = 8


def neg_expm1(u):
    series = jnp.ones_like(u)
    for k in range(11, 1, -1):
        series = 1.0 - series * u * (1.0 / k)
    return jnp.where(u < 0.5, u * series, 1.0 - jnp.exp(-u))


def block_kernel(
    layers, keys_hbm, vis_hbm, raw_hbm, taps_hbm, join_hbm, rates_hbm, out_ref,
    keys_ref, vis_ref, raw_ref, join_ref, rates_ref, load,
    stage, coords, edge_out, edge_in, rims, turned_rims, first_wide, first, weights, hidden, slab_hidden, slab_mixed,
    lifted, masks, joiner, powers, kept_forms, part_out, part_in, ends,
    edge_send, edge_recv, body_send, body_recv,
    mate_send, mate_recv, x_send, x_recv, y_send, y_recv, pass_send, pass_recv,
    part_send, part_recv, end_send, end_recv,
):
    joints, views, length = keys_ref.shape
    channels = raw_ref.shape[2]
    rows = taps_hbm.shape[1]
    states = rates_ref.shape[0]
    cams = 2
    group = 4
    count = layers * group
    pair = 2 * rows
    wide = length + LANES
    f32, bf16 = jnp.float32, jnp.bfloat16
    y = lax.axis_index("cam")
    i = lax.axis_index("tm")
    z = i // group
    l = i % group
    x = l // 2
    c = l % 2
    mate = z * group + 2 * x + 1 - c
    across = z * group + 2 * (1 - x) + c
    columns = (2 * x + 1 - c, 2 * (1 - x) + 1 - c)
    bent = x == c
    step = jnp.where(bent, jnp.where(c == 0, -1, 1), 0)
    spans = (i > 0) & (i < count - 1)

    barrier = pltpu.get_barrier_semaphore()

    def greet(cam, tm):
        pl.semaphore_signal(barrier, inc=1, device_id=(cam, tm), device_id_type=MESH)

    for d in range(1, count):
        greet(y, lax.rem(i + d, count))
    for d in range(layers):
        greet(1 - y, d * group + l)

    own_taps = weights.at[x, :, pl.ds(pl.multiple_of(c * rows, rows), rows), :]
    loads = [
        pltpu.make_async_copy(src, dst, load.at[n])
        for n, (src, dst) in enumerate(
            (
                (keys_hbm, keys_ref), (vis_hbm, vis_ref), (taps_hbm, own_taps),
                (raw_hbm, raw_ref), (rates_hbm, rates_ref), (join_hbm, join_ref),
            )
        )
    ]
    for copy in loads:
        copy.start()
    stage[...] = jnp.zeros_like(stage)
    loads[0].wait()
    loads[1].wait()
    for v in range(views):
        stage[pl.ds(v * joints, joints), :] = (keys_ref[:, v, :].astype(f32) - 2048.0) / 2048.0
        stage[pl.ds(views * joints + v, 1), :] = vis_ref[pl.ds(y * views + v, 1), :].astype(f32)
    coords[z] = stage[...].astype(bf16)
    rim = jnp.concatenate([stage[:, length - LANES : length], stage[:, 0:LANES]], axis=1)
    rim = jnp.concatenate([rim, jnp.zeros((LANES - DEPTH, 2 * LANES), f32)], axis=0)
    edge_out[...] = rim.T[LANES - 8 : LANES + 8].astype(bf16)
    edge_in[2, z] = edge_out[...]

    @pl.when(bent)
    def _():
        edge_in[1, jnp.where(c == 0, layers - 1, 0)] = jnp.zeros((16, LANES), bf16)

    loads[2].wait()
    pl.semaphore_wait(barrier, count - 1 + layers)

    def remote(src, dst, send_sem, recv_sem, cam, tm):
        return pltpu.make_async_remote_copy(
            src_ref=src, dst_ref=dst, send_sem=send_sem, recv_sem=recv_sem,
            device_id=(cam, tm), device_id_type=MESH,
        )

    def edge_copy(column, origin, target, n):
        return remote(
            edge_out, edge_in.at[column, origin], edge_send.at[n],
            edge_recv.at[column * layers + origin], y, target,
        )

    def edge_sends(act):
        for d in range(layers):
            act(edge_copy(0, z, d * group + columns[0], d))
            if d > 0:
                peer = lax.rem(z + d, layers)
                act(edge_copy(2, z, peer * group + l, 2 * layers + d))

            @pl.when(spans)
            def _():
                act(edge_copy(1, z, d * group + columns[1], layers + d))

    def body_copy(origin, target):
        return remote(
            coords.at[origin], coords.at[origin], body_send.at[target], body_recv.at[origin],
            y, target * group + l,
        )

    def source(k):
        if k == 0:
            return z
        if k == 1:
            return jnp.where(z < layers - 1, z + 1, z - 1)
        if k == 2:
            return jnp.where(z == 0, 2, z - 1 - jnp.where(z == layers - 1, 1, 0))
        return jnp.where(z < 2, 3, 0)

    sources = [source(k) for k in range(layers)]

    quarter = rows // 4
    x_parts = ((y, 0, 2), (y, 2, 1), (y, 3, 1), (2, 0, 4), (1 - y, 3, 1))
    y_parts = ((1 - y, 0, 2), (1 - y, 2, 1))

    def block(ref, part, base):
        o, start, size = part
        return ref.at[o, pl.ds(pl.multiple_of(base + start * quarter, quarter), size * quarter), :]

    def mate_copy(cs):
        at = weights.at[x, :, pl.ds(pl.multiple_of(cs * rows, rows), rows), :]
        return remote(at, at, mate_send, mate_recv, y, mate)

    def x_copy(n, first):
        at = block(weights.at[x if first else 1 - x], x_parts[n], c * rows)
        return remote(at, at, x_send.at[n], x_recv.at[n], y, across)

    def y_copy(n, first):
        part = x_parts[n] if first else y_parts[n]
        at = block(weights.at[1 - x], part, c * rows)
        return remote(at, at, y_send.at[n], y_recv.at[n], 1 - y, i)

    def pass_copy(n, cs):
        at = block(weights.at[1 - x], (x_parts + y_parts)[n], cs * rows)
        return remote(at, at, pass_send.at[n], pass_recv.at[n], y, mate)

    x_copy(0, True).start()
    edge_sends(lambda copy: copy.start())
    body_copy(z, sources[1]).start()
    x_copy(1, True).start()
    body_copy(z, sources[2]).start()
    mate_copy(c).start()
    for n in range(2, 5):
        x_copy(n, True).start()
    body_copy(z, sources[3]).start()

    def serve_x(n):
        x_copy(n, False).wait_recv()
        if n < 2:
            y_copy(n, True).start()
        pass_copy(n, c).start()

    def serve_y(n):
        y_copy(n, False).wait_recv()
        pass_copy(5 + n, c).start()

    loads[3].wait()
    first_wide[...] = jnp.zeros_like(first_wide)
    for o in range(3):
        first_wide[pl.ds(o * DEPTH, joints), :] = raw_ref[o].astype(f32)
    turned = first_wide[...].T
    first[0] = turned[:, : 3 * DEPTH].astype(bf16)
    first[1] = pltpu.roll(turned, joints, 1)[:, : 3 * DEPTH].astype(bf16)
    loads[5].wait()
    for n, xs in ((0, x), (1, 1 - x)):
        joiner[:, n * pair : (n + 1) * pair] = join_ref[
            :, pl.ds(pl.multiple_of(z * 2 * pair + xs * pair, pair), pair)
        ]

    rim_lane = lax.broadcasted_iota(jnp.int32, (3 * DEPTH, LANES), 1)
    body_lane = lax.broadcasted_iota(jnp.int32, (DEPTH, length), 1)
    rims[...] = jnp.zeros_like(rims)

    def gather_rim(k):
        s = sources[k]
        if k > 0:
            edge_copy(2, s, i, 0).wait_recv()
        edge_copy(0, s, i, 0).wait_recv()
        ahead = s + step
        inside = (ahead >= 0) & (ahead < layers)

        @pl.when(inside)
        def _():
            edge_copy(1, ahead, i, 0).wait_recv()

        near = edge_in[0, s].astype(f32)
        away = edge_in[1, lax.rem(ahead + layers, layers)].astype(f32)
        away = jnp.where(inside, away, 0.0)
        own = edge_in[2, s].astype(f32)
        right = jnp.where(c == 0, near, away)
        left = jnp.where(c == 0, away, near)
        rims[4 * SLOT * k : 4 * SLOT * (k + 1), :] = jnp.concatenate(
            [left[0:8], own[8:16], own[0:8], right[8:16]], axis=0
        )

    def expand_shard(k):
        if k > 0:
            body_copy(sources[k], z).wait_recv()
        rim = turned_rims[min(k, 1), 0:DEPTH, :]
        at = 4 * SLOT * k
        e = coords[sources[k]].astype(f32)
        masks[k] = e[DEPTH - 8 : DEPTH]
        before = jnp.where(body_lane == 0, rim[:, at + 7 : at + 8], pltpu.roll(e, 1, 1))
        after = jnp.where(
            body_lane == length - 1, rim[:, at + 24 : at + 25], pltpu.roll(e, length - 1, 1)
        )
        body = jnp.concatenate([before, e, after], axis=0).astype(bf16)
        for v in range(views):
            h = jnp.dot(first[v], body, preferred_element_type=f32)
            hidden[k, v] = jnp.maximum(h, 0.0).astype(bf16)

    own_rows = weights.at[x]
    other_rows = weights.at[1 - x]

    def lift(a, n, k, v, xs):
        rest = hidden[k, v, pl.ds(pl.multiple_of(z * 2 * pair + xs * pair, pair), pair), :]
        at = 4 * SLOT * k
        cols = slice(v * LANES, (v + 1) * LANES)
        older = pltpu.roll(slab_mixed[min(k, 1), n, 0:pair, cols], (2 * LANES - 8 - at) % LANES, 1)
        newer = pltpu.roll(slab_mixed[min(k, 1), n, 2 * pair :, cols], (LANES - 24 - at) % LANES, 1)
        left = pltpu.roll(jnp.concatenate([a[0:pair], older], axis=1), DILATION_STEP, 1)
        right = pltpu.roll(
            jnp.concatenate([a[2 * pair :], newer], axis=1), wide - DILATION_STEP, 1
        )
        acc = left[:, :length] + a[pair : 2 * pair] + right[:, :length]
        return (rest.astype(f32) + jnp.maximum(acc, 0.0)).astype(bf16)

    def early(k):
        w = own_rows[...].reshape(3 * pair, channels)
        for v in range(views):
            a = jnp.dot(w, hidden[k, v], preferred_element_type=f32)
            lifted[k, v, 0:pair] = lift(a, 0, k, v, x)

    def finish(k):
        w = other_rows[...].reshape(3 * pair, channels)
        total = jnp.zeros((cams * states, length), f32)
        for v in range(views):
            b = jnp.dot(w, hidden[k, v], preferred_element_type=f32)
            lifted[k, v, pair : 2 * pair] = lift(b, 1, k, v, 1 - x)
            at = views * joints % 8 + v
            total = total + masks[k, at : at + 1, :] * jnp.dot(
                joiner[...], lifted[k, v], preferred_element_type=f32
            )
        for cam in range(cams):
            part_out[k, cam] = total[cam * states : (cam + 1) * states].astype(bf16)
        if k > 0:
            for cam in range(cams):
                part_copy(k, cam, sources[k] * group + l).start()
        else:
            part_copy(0, 1 - y, i).start()
            part_in[z * cams + y] = part_out[0, y]

    def part_copy(k, cam, tm):
        return remote(
            part_out.at[k, cam], part_in.at[z * cams + y], part_send.at[k * cams + cam],
            part_recv.at[z * cams + y], cam, tm,
        )

    lane = lax.broadcasted_iota(jnp.int32, (states, length), 1)

    bits = length.bit_length() - 1

    def place(step, reverse):
        turn = length - step if reverse else step
        return turn, (lane < length - step) if reverse else (lane >= step)

    def products(prod, reverse):
        for k in range(bits):
            powers[int(reverse) * bits + k] = prod
            turn, fits = place(1 << k, reverse)
            prod = prod * jnp.where(fits, pltpu.roll(prod, turn, 1), 1.0)
        return prod

    def scan(value, reverse):
        for k in range(bits):
            turn, fits = place(1 << k, reverse)
            moved = jnp.where(fits, pltpu.roll(value, turn, 1), 0.0)
            value = value + powers[int(reverse) * bits + k] * moved
        return value

    loads[4].wait()
    rates = rates_ref[...]
    decay = jnp.exp(-rates)
    energy = neg_expm1(2.0 * rates)
    kept_forms[0] = products(decay, False)
    kept_forms[1] = products(decay, True)
    kept_forms[2] = scan(energy * kept_forms[0], True)
    kept_forms[3] = energy
    kept_forms[4] = jnp.sqrt(energy)

    def slab(part):
        members = range(1) if part == 0 else range(1, layers)
        for k in members:
            gather_rim(k)
        rim = rims[...].T
        turned_rims[part] = rim
        rim = rim[0:DEPTH, :]
        tile = jnp.concatenate([pltpu.roll(rim, 1, 1), rim, pltpu.roll(rim, LANES - 1, 1)], axis=0)
        for k in members:
            shard = sources[k] * group + l
            at = 4 * SLOT * k
            begins = (shard == 0) & (rim_lane >= at) & (rim_lane < at + 8)
            ends_here = (shard == count - 1) & (rim_lane >= at + 24) & (rim_lane < at + 32)
            tile = jnp.where(begins | ends_here, 0.0, tile)
        tile = tile.astype(bf16)
        for v in range(views):
            h = jnp.dot(first[v], tile, preferred_element_type=f32)
            slab_hidden[part, :, v * LANES : (v + 1) * LANES] = jnp.maximum(h, 0.0).astype(bf16)

    def slab_mix(part, n):
        w = (other_rows if n else own_rows)[...].reshape(3 * pair, channels)
        slab_mixed[part, n] = jnp.dot(w, slab_hidden[part], preferred_element_type=f32)

    slab(0)
    expand_shard(0)
    serve_x(0)
    mate_copy(1 - c).wait_recv()
    slab_mix(0, 0)
    serve_x(1)
    early(0)
    serve_x(2)
    slab(1)
    slab_mix(1, 0)
    expand_shard(1)
    early(1)
    serve_x(3)
    serve_y(0)
    serve_x(4)
    serve_y(1)
    expand_shard(2)
    early(2)
    expand_shard(3)
    early(3)
    for n in range(7):
        pass_copy(n, 1 - c).wait_recv()
    slab_mix(0, 1)
    slab_mix(1, 1)
    for k in range(layers - 1, -1, -1):
        finish(k)

    seen = jnp.sum(vis_ref[...].astype(f32), axis=0, keepdims=True)
    members = cams * layers
    me = z * cams + y
    for d in range(1, members):
        other = lax.rem(me + d, members)
        remote(
            part_in.at[other], part_in.at[other], part_send.at[0], part_recv.at[other],
            other % cams, (other // cams) * group + l,
        ).wait_recv()
    summed = part_in[0].astype(f32)
    for p in range(1, members):
        summed = summed + part_in[p].astype(f32)
    joined = summed / jnp.maximum(seen, 1.0)

    local = scan(kept_forms[4] * joined, False)
    back = scan(kept_forms[3] * local, True)
    prod_fwd, prod_back, through = kept_forms[0], kept_forms[1], kept_forms[2]

    square = lax.broadcasted_iota(jnp.int32, (states, LANES), 1)
    packed = jnp.where(
        square == 0,
        prod_fwd[:, length - 1 : length],
        jnp.where(
            square == 1,
            local[:, length - 1 : length],
            jnp.where(square == 2, back[:, 0:1], through[:, 0:1]),
        ),
    )
    packed = jnp.concatenate([packed, jnp.zeros((LANES - states, LANES), f32)], axis=0)
    ends[i] = packed.T[0:8]

    def end_copy(origin, target, sem):
        return remote(ends.at[origin], ends.at[origin], sem, end_recv.at[origin], y, target)

    for k in range(layers - 1, -1, -1):
        for d in range(group):
            if k + d > 0:
                target = sources[k] * group + lax.rem(l + d, group)
                end_copy(i, target, end_send.at[target]).start()
    for d in range(1, count):
        origin = lax.rem(i + count - d, count)
        end_copy(origin, origin, end_send.at[origin]).wait_recv()

    entry = jnp.zeros((1, LANES), f32)
    carried = entry
    entries = []
    for j in range(count):
        entries.append(entry)
        carried = jnp.where(j == i, entry, carried)
        entry = ends[j, 0:1] * entry + ends[j, 1:2]
    state = jnp.zeros((1, LANES), f32)
    returned = state
    for j in range(count - 1, -1, -1):
        returned = jnp.where(j == i, state, returned)
        state = ends[j, 0:1] * state + ends[j, 2:3] + ends[j, 3:4] * entries[j]
    both = jnp.concatenate([carried, returned, jnp.zeros((LANES - 2, LANES), f32)], axis=0).T
    out_ref[...] = back + through * both[0:states, 0:1] + prod_back * both[0:states, 1:2]

    edge_sends(lambda copy: copy.wait_send())
    for k in range(1, layers):
        body_copy(z, sources[k]).wait_send()
    mate_copy(c).wait_send()
    for n in range(5):
        x_copy(n, True).wait_send()
    for n in range(2):
        y_copy(n, True).wait_send()
    for n in range(7):
        pass_copy(n, c).wait_send()

    for k in range(1, layers):
        for cam in range(cams):
            part_copy(k, cam, sources[k] * group + l).wait_send()
    part_copy(0, 1 - y, i).wait_send()
    for d in range(1, count):
        target = lax.rem(i + d, count)
        end_copy(i, target, end_send.at[target]).wait_send()


def block_body(cams, count, group):
    layers = count // group

    def run(keypoints, visibility, expand_weight, dilated_tap_weight, join_weight, decay_rates):
        views, joints, length = keypoints.shape
        channels = expand_weight.shape[2]
        rows = dilated_tap_weight.shape[0]
        states = decay_rates.shape[0]
        keys = jnp.transpose(keypoints, (1, 0, 2))
        taps = jnp.transpose(dilated_tap_weight, (1, 0, 2))
        wide = length + LANES
        bits = length.bit_length() - 1
        dma, vmem = (pltpu.SemaphoreType.DMA, pltpu.VMEM)
        f32, bf16 = jnp.float32, jnp.bfloat16
        sems = [3 * layers] * 2 + [layers] * 2 + [0] * 2 + [5, 5, 2, 2, 7, 7] + [cams * layers] * 2 + [count] * 2
        return pl.pallas_call(
            functools.partial(block_kernel, layers),
            out_shape=jax.ShapeDtypeStruct(decay_rates.shape, f32),
            in_specs=[pl.BlockSpec(memory_space=pl.ANY)] * 6,
            out_specs=pl.BlockSpec(memory_space=pltpu.VMEM),
            scratch_shapes=[
                vmem(keys.shape, jnp.int32),
                vmem(visibility.shape, jnp.int32),
                vmem(expand_weight.shape, bf16),
                vmem((states * cams, channels), bf16),
                vmem(decay_rates.shape, f32),
                dma((6,)),
                vmem((DEPTH, length), f32),
                vmem((layers, DEPTH, length), bf16),
                vmem((16, LANES), bf16),
                vmem((3, layers, 16, LANES), bf16),
                vmem((LANES, LANES), f32),
                vmem((2, LANES, LANES), f32),
                vmem((2 * LANES, channels), f32),
                vmem((views, channels, 3 * DEPTH), bf16),
                vmem((2, 3, 2 * rows, channels), bf16),
                vmem((layers, views, channels, length), bf16),
                vmem((2, channels, views * LANES), bf16),
                vmem((2, 2, 6 * rows, views * LANES), f32),
                vmem((layers, views, 4 * rows, length), bf16),
                vmem((layers, 8, length), f32),
                vmem((cams * states, 4 * rows), bf16),
                vmem((2 * bits, states, length), f32),
                vmem((5, states, length), f32),
                vmem((layers, cams, states, length), bf16),
                vmem((cams * layers, states, length), bf16),
                vmem((count, 8, LANES), f32),
            ]
            + [dma((n,)) if n else dma for n in sems],
            compiler_params=pltpu.CompilerParams(
                collective_id=0, has_side_effects=True, vmem_limit_bytes=58 * 1024 * 1024
            ),
        )(keys, visibility, expand_weight, taps, join_weight.T, decay_rates)

    return run


def solution(mesh):
    cams, count = mesh.shape["cam"], mesh.shape["tm"]
    group = 4
    fits = count % group == 0 and cams == 2 and count == 4 * group
    return jax.shard_map(
        block_body(cams, count, group) if fits else body,
        mesh=mesh,
        in_specs=(
            P("cam", None, "tm"),
            P(None, "tm"),
            P(),
            P("tm", None, None),
            P(),
            P("cam", "tm"),
        ),
        out_specs=P("cam", "tm"),
        check_vma=False,
    )
```

```python
import functools

import jax
import jax.numpy as jnp
from jax import lax
from jax.experimental import pallas as pl
from jax.experimental.pallas import tpu as pltpu
from jax.sharding import PartitionSpec as P

DILATION_STEP = 3
MESH = pl.DeviceIdType.MESH


def with_halo(array, sides, width):
    for axis, dim in sides:
        count, length = (lax.axis_size(axis), array.shape[dim])
        up = [(i, (i + 1) % count) for i in range(count - 1)]
        down = [(j, i) for i, j in up]
        last = lax.slice_in_dim(array, length - width, length, axis=dim)
        initial = lax.slice_in_dim(array, 0, width, axis=dim)
        before = lax.ppermute(last, axis, up)
        after = lax.ppermute(initial, axis, down)
        array = jnp.concatenate([before, array, after], axis=dim)
    return array


def entering(part, axis, combine, identity, reverse):
    count = lax.axis_size(axis)
    place = lax.axis_index(axis)
    ahead = count - 1 - place if reverse else place
    gathered = jax.tree.map(lambda a: lax.all_gather(a, axis), part)
    state = jax.tree.map(lambda a, e: jnp.zeros_like(a) + jnp.asarray(e, a.dtype), part, identity)

    def one(turn, state):
        source = count - 1 - turn if reverse else turn
        return combine(
            state, jax.tree.map(lambda a: lax.dynamic_index_in_dim(a, source, 0, False), gathered)
        )

    return lax.fori_loop(0, ahead, one, state)


def expand(widened_output, expand_weight, width):
    total = None
    for shift_amount in range(3):
        term = jnp.einsum(
            "vjt,jc->vtc",
            widened_output[:, :, shift_amount : shift_amount + width],
            expand_weight[shift_amount],
            preferred_element_type=jnp.float32,
        )
        total = term if total is None else total + term
    return jax.nn.relu(total).astype(jnp.bfloat16)


def dilate(padded_input, hidden_start0, weight_rows):
    count_of_frames = hidden_start0.shape[1]
    total = None
    for shift_amount in range(3):
        term = jnp.einsum(
            "vti,ni->vtn",
            padded_input[
                :, shift_amount * DILATION_STEP : shift_amount * DILATION_STEP + count_of_frames
            ],
            weight_rows[:, shift_amount],
            preferred_element_type=jnp.float32,
        )
        total = term if total is None else total + term
    residual = hidden_start0.astype(jnp.float32)
    return (residual + jax.nn.relu(total)).astype(jnp.bfloat16)


def chain(earlier, latter):
    return (earlier[0] * latter[0], latter[0] * earlier[1] + latter[1])


def body(keypoints, visibility, expand_weight, dilated_tap_weight, join_weight, decay_rates):
    view_count = keypoints.shape[0]
    count_of_frames = keypoints.shape[2]
    coords = ((keypoints.astype(jnp.float32) - 2048.0) / 2048.0).astype(jnp.bfloat16)
    widened_output = with_halo(coords, (("tm", 2),), 1)
    hidden_start0 = expand(widened_output, expand_weight, count_of_frames)
    padded_input = with_halo(hidden_start0, (("tm", 1),), DILATION_STEP)
    hidden1 = dilate(
        padded_input, hidden_start0, lax.all_gather(dilated_tap_weight, "tm", axis=0, tiled=True)
    )
    own_mask = lax.dynamic_slice_in_dim(
        visibility, lax.axis_index("cam") * view_count, view_count, 0
    )
    masked = hidden1 * own_mask[:, :, None].astype(jnp.bfloat16)
    state_rows = decay_rates.shape[0]
    total = lax.psum_scatter(
        jnp.einsum("vti,is->st", masked, join_weight, preferred_element_type=jnp.float32).astype(
            jnp.bfloat16
        ),
        "cam",
        scatter_dimension=0,
        tiled=True,
    ).astype(jnp.float32)
    seen = jnp.sum(visibility.astype(jnp.float32), axis=0)
    joined = total / jnp.maximum(seen, 1.0)[None, :]
    decay = jnp.exp(-decay_rates)
    energy = -jnp.expm1(-2.0 * decay_rates)
    drive = jnp.sqrt(energy)
    prod_fwd, local_fwd = lax.associative_scan(chain, (decay, drive * joined), axis=1)
    ones_vec = jnp.ones((state_rows,), jnp.float32)
    zeros_vec = jnp.zeros((state_rows,), jnp.float32)
    carried = entering(
        (prod_fwd[:, -1], local_fwd[:, -1]), "tm", chain, (ones_vec, zeros_vec), False
    )
    filtered = local_fwd + prod_fwd * carried[1][:, None]
    prod_back, local_back = lax.associative_scan(
        chain, (decay, energy * filtered), axis=1, reverse=True
    )
    returned = entering(
        (prod_back[:, 0], local_back[:, 0]), "tm", chain, (ones_vec, zeros_vec), True
    )
    smoothed = local_back + prod_back * returned[1][:, None]
    return smoothed

LANES = 128
DEPTH = 72
SLOT = 8
RADIX = 4


def neg_expm1(u):
    series = jnp.ones_like(u)
    for k in range(11, 1, -1):
        series = 1.0 - series * u * (1.0 / k)
    return jnp.where(u < 0.5, u * series, 1.0 - jnp.exp(-u))


def block_kernel(
    layers, keys_hbm, vis_hbm, raw_hbm, taps_hbm, join_hbm, rates_hbm, out_ref,
    keys_ref, vis_ref, raw_ref, join_ref, rates_ref, load,
    stage, coords, edge_out, edge_in, rims, turned_rims, first_wide, first, weights, hidden, slab_hidden, slab_mixed,
    lifted, masks, joiner, powers, kept_forms, part_out, part_in, ends,
    edge_send, edge_recv, body_send, body_recv,
    mate_send, mate_recv, x_send, x_recv, y_send, y_recv, pass_send, pass_recv,
    part_send, part_recv, end_send, end_recv,
):
    joints, views, length = keys_ref.shape
    channels = raw_ref.shape[2]
    rows = taps_hbm.shape[1]
    states = rates_ref.shape[0]
    cams = 2
    group = 4
    count = layers * group
    pair = 2 * rows
    wide = length + LANES
    f32, bf16 = jnp.float32, jnp.bfloat16
    y = lax.axis_index("cam")
    i = lax.axis_index("tm")
    z = i // group
    l = i % group
    x = l // 2
    c = l % 2
    mate = z * group + 2 * x + 1 - c
    across = z * group + 2 * (1 - x) + c
    columns = (2 * x + 1 - c, 2 * (1 - x) + 1 - c)
    bent = x == c
    step = jnp.where(bent, jnp.where(c == 0, -1, 1), 0)
    spans = (i > 0) & (i < count - 1)

    barrier = pltpu.get_barrier_semaphore()

    def greet(cam, tm):
        pl.semaphore_signal(barrier, inc=1, device_id=(cam, tm), device_id_type=MESH)

    for d in range(1, count):
        greet(y, lax.rem(i + d, count))
    for d in range(layers):
        greet(1 - y, d * group + l)

    own_taps = weights.at[x, :, pl.ds(pl.multiple_of(c * rows, rows), rows), :]
    loads = [
        pltpu.make_async_copy(src, dst, load.at[n])
        for n, (src, dst) in enumerate(
            (
                (keys_hbm, keys_ref), (vis_hbm, vis_ref), (taps_hbm, own_taps),
                (raw_hbm, raw_ref), (rates_hbm, rates_ref), (join_hbm, join_ref),
            )
        )
    ]
    for copy in loads:
        copy.start()
    stage[...] = jnp.zeros_like(stage)
    loads[0].wait()
    loads[1].wait()
    for v in range(views):
        stage[pl.ds(v * joints, joints), :] = (keys_ref[:, v, :].astype(f32) - 2048.0) / 2048.0
        stage[pl.ds(views * joints + v, 1), :] = vis_ref[pl.ds(y * views + v, 1), :].astype(f32)
    coords[z] = stage[...].astype(bf16)
    rim = jnp.concatenate([stage[:, length - LANES : length], stage[:, 0:LANES]], axis=1)
    rim = jnp.concatenate([rim, jnp.zeros((LANES - DEPTH, 2 * LANES), f32)], axis=0)
    edge_out[...] = rim.T[LANES - 8 : LANES + 8].astype(bf16)
    edge_in[2, z] = edge_out[...]

    @pl.when(bent)
    def _():
        edge_in[1, jnp.where(c == 0, layers - 1, 0)] = jnp.zeros((16, LANES), bf16)

    loads[2].wait()
    pl.semaphore_wait(barrier, count - 1 + layers)

    def remote(src, dst, send_sem, recv_sem, cam, tm):
        return pltpu.make_async_remote_copy(
            src_ref=src, dst_ref=dst, send_sem=send_sem, recv_sem=recv_sem,
            device_id=(cam, tm), device_id_type=MESH,
        )

    def edge_copy(column, origin, target, n):
        return remote(
            edge_out, edge_in.at[column, origin], edge_send.at[n],
            edge_recv.at[column * layers + origin], y, target,
        )

    def edge_sends(act):
        for d in range(layers):
            act(edge_copy(0, z, d * group + columns[0], d))
            if d > 0:
                peer = lax.rem(z + d, layers)
                act(edge_copy(2, z, peer * group + l, 2 * layers + d))

            @pl.when(spans)
            def _():
                act(edge_copy(1, z, d * group + columns[1], layers + d))

    def body_copy(origin, target):
        return remote(
            coords.at[origin], coords.at[origin], body_send.at[target], body_recv.at[origin],
            y, target * group + l,
        )

    def source(k):
        if k == 0:
            return z
        if k == 1:
            return jnp.where(z < layers - 1, z + 1, z - 1)
        if k == 2:
            return jnp.where(z == 0, 2, z - 1 - jnp.where(z == layers - 1, 1, 0))
        return jnp.where(z < 2, 3, 0)

    sources = [source(k) for k in range(layers)]

    quarter = rows // 4
    x_parts = ((y, 0, 2), (y, 2, 1), (y, 3, 1), (2, 0, 4), (1 - y, 3, 1))
    y_parts = ((1 - y, 0, 2), (1 - y, 2, 1))

    def block(ref, part, base):
        o, start, size = part
        return ref.at[o, pl.ds(pl.multiple_of(base + start * quarter, quarter), size * quarter), :]

    def mate_copy(cs):
        at = weights.at[x, :, pl.ds(pl.multiple_of(cs * rows, rows), rows), :]
        return remote(at, at, mate_send, mate_recv, y, mate)

    def x_copy(n, first):
        at = block(weights.at[x if first else 1 - x], x_parts[n], c * rows)
        return remote(at, at, x_send.at[n], x_recv.at[n], y, across)

    def y_copy(n, first):
        part = x_parts[n] if first else y_parts[n]
        at = block(weights.at[1 - x], part, c * rows)
        return remote(at, at, y_send.at[n], y_recv.at[n], 1 - y, i)

    def pass_copy(n, cs):
        at = block(weights.at[1 - x], (x_parts + y_parts)[n], cs * rows)
        return remote(at, at, pass_send.at[n], pass_recv.at[n], y, mate)

    x_copy(0, True).start()
    edge_sends(lambda copy: copy.start())
    body_copy(z, sources[1]).start()
    x_copy(1, True).start()
    body_copy(z, sources[2]).start()
    mate_copy(c).start()
    for n in range(2, 5):
        x_copy(n, True).start()
    body_copy(z, sources[3]).start()

    def serve_x(n):
        x_copy(n, False).wait_recv()
        if n < 2:
            y_copy(n, True).start()
        pass_copy(n, c).start()

    def serve_y(n):
        y_copy(n, False).wait_recv()
        pass_copy(5 + n, c).start()

    loads[3].wait()
    first_wide[...] = jnp.zeros_like(first_wide)
    for o in range(3):
        first_wide[pl.ds(o * DEPTH, joints), :] = raw_ref[o].astype(f32)
    turned = first_wide[...].T
    first[0] = turned[:, : 3 * DEPTH].astype(bf16)
    first[1] = pltpu.roll(turned, joints, 1)[:, : 3 * DEPTH].astype(bf16)
    loads[5].wait()
    for n, xs in ((0, x), (1, 1 - x)):
        joiner[:, n * pair : (n + 1) * pair] = join_ref[
            :, pl.ds(pl.multiple_of(z * 2 * pair + xs * pair, pair), pair)
        ]

    rim_lane = lax.broadcasted_iota(jnp.int32, (3 * DEPTH, LANES), 1)
    body_lane = lax.broadcasted_iota(jnp.int32, (DEPTH, length), 1)
    rims[...] = jnp.zeros_like(rims)

    def gather_rim(k):
        s = sources[k]
        if k > 0:
            edge_copy(2, s, i, 0).wait_recv()
        edge_copy(0, s, i, 0).wait_recv()
        ahead = s + step
        inside = (ahead >= 0) & (ahead < layers)

        @pl.when(inside)
        def _():
            edge_copy(1, ahead, i, 0).wait_recv()

        near = edge_in[0, s].astype(f32)
        away = edge_in[1, lax.rem(ahead + layers, layers)].astype(f32)
        away = jnp.where(inside, away, 0.0)
        own = edge_in[2, s].astype(f32)
        right = jnp.where(c == 0, near, away)
        left = jnp.where(c == 0, away, near)
        rims[4 * SLOT * k : 4 * SLOT * (k + 1), :] = jnp.concatenate(
            [left[0:8], own[8:16], own[0:8], right[8:16]], axis=0
        )

    def expand_shard(k):
        if k > 0:
            body_copy(sources[k], z).wait_recv()
        rim = turned_rims[min(k, 1), 0:DEPTH, :]
        at = 4 * SLOT * k
        e = coords[sources[k]].astype(f32)
        masks[k] = e[DEPTH - 8 : DEPTH]
        before = jnp.where(body_lane == 0, rim[:, at + 7 : at + 8], pltpu.roll(e, 1, 1))
        after = jnp.where(
            body_lane == length - 1, rim[:, at + 24 : at + 25], pltpu.roll(e, length - 1, 1)
        )
        body = jnp.concatenate([before, e, after], axis=0).astype(bf16)
        for v in range(views):
            h = jnp.dot(first[v], body, preferred_element_type=f32)
            hidden[k, v] = jnp.maximum(h, 0.0).astype(bf16)

    own_rows = weights.at[x]
    other_rows = weights.at[1 - x]

    def lift(a, n, k, v, xs):
        rest = hidden[k, v, pl.ds(pl.multiple_of(z * 2 * pair + xs * pair, pair), pair), :]
        at = 4 * SLOT * k
        cols = slice(v * LANES, (v + 1) * LANES)
        older = pltpu.roll(slab_mixed[min(k, 1), n, 0:pair, cols], (2 * LANES - 8 - at) % LANES, 1)
        newer = pltpu.roll(slab_mixed[min(k, 1), n, 2 * pair :, cols], (LANES - 24 - at) % LANES, 1)
        left = pltpu.roll(jnp.concatenate([a[0:pair], older], axis=1), DILATION_STEP, 1)
        right = pltpu.roll(
            jnp.concatenate([a[2 * pair :], newer], axis=1), wide - DILATION_STEP, 1
        )
        acc = left[:, :length] + a[pair : 2 * pair] + right[:, :length]
        return (rest.astype(f32) + jnp.maximum(acc, 0.0)).astype(bf16)

    def early(k):
        w = own_rows[...].reshape(3 * pair, channels)
        for v in range(views):
            a = jnp.dot(w, hidden[k, v], preferred_element_type=f32)
            lifted[k, v, 0:pair] = lift(a, 0, k, v, x)

    def late(k, v):
        w = other_rows[...].reshape(3 * pair, channels)
        b = jnp.dot(w, hidden[k, v], preferred_element_type=f32)
        lifted[k, v, pair : 2 * pair] = lift(b, 1, k, v, 1 - x)

    def join(k):
        total = jnp.zeros((cams * states, length), f32)
        for v in range(views):
            at = views * joints % 8 + v
            total = total + masks[k, at : at + 1, :] * jnp.dot(
                joiner[...], lifted[k, v], preferred_element_type=f32
            )
        for cam in range(cams):
            part_out[k, cam] = total[cam * states : (cam + 1) * states].astype(bf16)

    def give(k):
        if k > 0:
            for cam in range(cams):
                part_copy(k, cam, sources[k] * group + l).start()
        else:
            part_copy(0, 1 - y, i).start()
            part_in[z * cams + y] = part_out[0, y]

    def part_copy(k, cam, tm):
        return remote(
            part_out.at[k, cam], part_in.at[z * cams + y], part_send.at[k * cams + cam],
            part_recv.at[z * cams + y], cam, tm,
        )

    lane = lax.broadcasted_iota(jnp.int32, (states, length), 1)

    levels = []
    base = 1
    while base < length:
        levels.append([n * base for n in range(1, RADIX) if n * base < length])
        base *= RADIX

    def place(shift, reverse):
        turn = length - shift if reverse else shift
        return turn, (lane < length - shift) if reverse else (lane >= shift)

    def products(prod, reverse):
        at = int(reverse) * sum(map(len, levels))
        for shifts in levels:
            unit = prod
            for shift in shifts:
                turn, fits = place(shift, reverse)
                powers[at] = jnp.where(fits, prod, 0.0)
                at += 1
                prod = prod * jnp.where(fits, pltpu.roll(unit, turn, 1), 1.0)
        return prod

    def scan(value, reverse):
        at = int(reverse) * sum(map(len, levels))
        for shifts in levels:
            terms = [value]
            for shift in shifts:
                turn, _ = place(shift, reverse)
                terms.append(powers[at] * pltpu.roll(value, turn, 1))
                at += 1
            while len(terms) > 1:
                terms = [sum(terms[n : n + 2][1:], terms[n]) for n in range(0, len(terms), 2)]
            value = terms[0]
        return value

    loads[4].wait()
    rates = rates_ref[...]
    decay = jnp.exp(-rates)
    energy = neg_expm1(2.0 * rates)
    kept_forms[0] = products(decay, False)
    kept_forms[1] = products(decay, True)
    kept_forms[2] = scan(energy * kept_forms[0], True)
    kept_forms[3] = energy
    kept_forms[4] = jnp.sqrt(energy)

    def slab(part):
        members = range(1) if part == 0 else range(1, layers)
        for k in members:
            gather_rim(k)
        rim = rims[...].T
        turned_rims[part] = rim
        rim = rim[0:DEPTH, :]
        tile = jnp.concatenate([pltpu.roll(rim, 1, 1), rim, pltpu.roll(rim, LANES - 1, 1)], axis=0)
        for k in members:
            shard = sources[k] * group + l
            at = 4 * SLOT * k
            begins = (shard == 0) & (rim_lane >= at) & (rim_lane < at + 8)
            ends_here = (shard == count - 1) & (rim_lane >= at + 24) & (rim_lane < at + 32)
            tile = jnp.where(begins | ends_here, 0.0, tile)
        tile = tile.astype(bf16)
        for v in range(views):
            h = jnp.dot(first[v], tile, preferred_element_type=f32)
            slab_hidden[part, :, v * LANES : (v + 1) * LANES] = jnp.maximum(h, 0.0).astype(bf16)

    def slab_mix(part, n):
        w = (other_rows if n else own_rows)[...].reshape(3 * pair, channels)
        slab_mixed[part, n] = jnp.dot(w, slab_hidden[part], preferred_element_type=f32)

    slab(0)
    expand_shard(0)
    serve_x(0)
    mate_copy(1 - c).wait_recv()
    slab_mix(0, 0)
    serve_x(1)
    early(0)
    serve_x(2)
    slab(1)
    slab_mix(1, 0)
    expand_shard(1)
    early(1)
    serve_x(3)
    serve_y(0)
    serve_x(4)
    serve_y(1)
    expand_shard(2)
    early(2)
    expand_shard(3)
    early(3)
    for n in range(7):
        pass_copy(n, 1 - c).wait_recv()
    slab_mix(0, 1)
    slab_mix(1, 1)
    for k in range(layers - 1, -1, -1):
        late(k, 0)
        if k < layers - 1:
            join(k + 1)
            give(k + 1)
        late(k, 1)
    join(0)
    give(0)

    seen = jnp.sum(vis_ref[...].astype(f32), axis=0, keepdims=True)
    members = cams * layers
    me = z * cams + y
    for d in range(1, members):
        other = lax.rem(me + d, members)
        remote(
            part_in.at[other], part_in.at[other], part_send.at[0], part_recv.at[other],
            other % cams, (other // cams) * group + l,
        ).wait_recv()
    summed = part_in[0].astype(f32)
    for p in range(1, members):
        summed = summed + part_in[p].astype(f32)
    joined = summed / jnp.maximum(seen, 1.0)

    local = scan(kept_forms[4] * joined, False)
    back = scan(kept_forms[3] * local, True)
    prod_fwd, prod_back, through = kept_forms[0], kept_forms[1], kept_forms[2]

    square = lax.broadcasted_iota(jnp.int32, (states, LANES), 1)
    packed = jnp.where(
        square == 0,
        prod_fwd[:, length - 1 : length],
        jnp.where(
            square == 1,
            local[:, length - 1 : length],
            jnp.where(square == 2, back[:, 0:1], through[:, 0:1]),
        ),
    )
    packed = jnp.concatenate([packed, jnp.zeros((LANES - states, LANES), f32)], axis=0)
    ends[i] = packed.T[0:8]

    def end_copy(origin, target, sem):
        return remote(ends.at[origin], ends.at[origin], sem, end_recv.at[origin], y, target)

    for k in range(layers - 1, -1, -1):
        for d in range(group):
            if k + d > 0:
                target = sources[k] * group + lax.rem(l + d, group)
                end_copy(i, target, end_send.at[target]).start()
    for d in range(1, count):
        origin = lax.rem(i + count - d, count)
        end_copy(origin, origin, end_send.at[origin]).wait_recv()

    entry = jnp.zeros((1, LANES), f32)
    carried = entry
    entries = []
    for j in range(count):
        entries.append(entry)
        carried = jnp.where(j == i, entry, carried)
        entry = ends[j, 0:1] * entry + ends[j, 1:2]
    state = jnp.zeros((1, LANES), f32)
    returned = state
    for j in range(count - 1, -1, -1):
        returned = jnp.where(j == i, state, returned)
        state = ends[j, 0:1] * state + ends[j, 2:3] + ends[j, 3:4] * entries[j]
    both = jnp.concatenate([carried, returned, jnp.zeros((LANES - 2, LANES), f32)], axis=0).T
    out_ref[...] = back + through * both[0:states, 0:1] + prod_back * both[0:states, 1:2]

    edge_sends(lambda copy: copy.wait_send())
    for k in range(1, layers):
        body_copy(z, sources[k]).wait_send()
    mate_copy(c).wait_send()
    for n in range(5):
        x_copy(n, True).wait_send()
    for n in range(2):
        y_copy(n, True).wait_send()
    for n in range(7):
        pass_copy(n, c).wait_send()

    for k in range(1, layers):
        for cam in range(cams):
            part_copy(k, cam, sources[k] * group + l).wait_send()
    part_copy(0, 1 - y, i).wait_send()
    for d in range(1, count):
        target = lax.rem(i + d, count)
        end_copy(i, target, end_send.at[target]).wait_send()


def block_body(cams, count, group):
    layers = count // group

    def run(keypoints, visibility, expand_weight, dilated_tap_weight, join_weight, decay_rates):
        views, joints, length = keypoints.shape
        channels = expand_weight.shape[2]
        rows = dilated_tap_weight.shape[0]
        states = decay_rates.shape[0]
        keys = jnp.transpose(keypoints, (1, 0, 2))
        taps = jnp.transpose(dilated_tap_weight, (1, 0, 2))
        wide = length + LANES
        steps = 0
        base = 1
        while base < length:
            steps += sum(n * base < length for n in range(1, RADIX))
            base *= RADIX
        dma, vmem = (pltpu.SemaphoreType.DMA, pltpu.VMEM)
        f32, bf16 = jnp.float32, jnp.bfloat16
        sems = [3 * layers] * 2 + [layers] * 2 + [0] * 2 + [5, 5, 2, 2, 7, 7] + [cams * layers] * 2 + [count] * 2
        return pl.pallas_call(
            functools.partial(block_kernel, layers),
            out_shape=jax.ShapeDtypeStruct(decay_rates.shape, f32),
            in_specs=[pl.BlockSpec(memory_space=pl.ANY)] * 6,
            out_specs=pl.BlockSpec(memory_space=pltpu.VMEM),
            scratch_shapes=[
                vmem(keys.shape, jnp.int32),
                vmem(visibility.shape, jnp.int32),
                vmem(expand_weight.shape, bf16),
                vmem((states * cams, channels), bf16),
                vmem(decay_rates.shape, f32),
                dma((6,)),
                vmem((DEPTH, length), f32),
                vmem((layers, DEPTH, length), bf16),
                vmem((16, LANES), bf16),
                vmem((3, layers, 16, LANES), bf16),
                vmem((LANES, LANES), f32),
                vmem((2, LANES, LANES), f32),
                vmem((2 * LANES, channels), f32),
                vmem((views, channels, 3 * DEPTH), bf16),
                vmem((2, 3, 2 * rows, channels), bf16),
                vmem((layers, views, channels, length), bf16),
                vmem((2, channels, views * LANES), bf16),
                vmem((2, 2, 6 * rows, views * LANES), f32),
                vmem((layers, views, 4 * rows, length), bf16),
                vmem((layers, 8, length), f32),
                vmem((cams * states, 4 * rows), bf16),
                vmem((2 * steps, states, length), f32),
                vmem((5, states, length), f32),
                vmem((layers, cams, states, length), bf16),
                vmem((cams * layers, states, length), bf16),
                vmem((count, 8, LANES), f32),
            ]
            + [dma((n,)) if n else dma for n in sems],
            compiler_params=pltpu.CompilerParams(
                collective_id=0, has_side_effects=True, vmem_limit_bytes=58 * 1024 * 1024
            ),
        )(keys, visibility, expand_weight, taps, join_weight.T, decay_rates)

    return run


def solution(mesh):
    cams, count = mesh.shape["cam"], mesh.shape["tm"]
    group = 4
    fits = count % group == 0 and cams == 2 and count == 4 * group
    return jax.shard_map(
        block_body(cams, count, group) if fits else body,
        mesh=mesh,
        in_specs=(
            P("cam", None, "tm"),
            P(None, "tm"),
            P(),
            P("tm", None, None),
            P(),
            P("cam", "tm"),
        ),
        out_specs=P("cam", "tm"),
        check_vma=False,
    )
```

```python
import functools

import jax
import jax.numpy as jnp
from jax import lax
from jax.experimental import pallas as pl
from jax.experimental.pallas import tpu as pltpu
from jax.sharding import PartitionSpec as P

DILATION_STEP = 3
MESH = pl.DeviceIdType.MESH


def with_halo(array, sides, width):
    for axis, dim in sides:
        count, length = (lax.axis_size(axis), array.shape[dim])
        up = [(i, (i + 1) % count) for i in range(count - 1)]
        down = [(j, i) for i, j in up]
        last = lax.slice_in_dim(array, length - width, length, axis=dim)
        initial = lax.slice_in_dim(array, 0, width, axis=dim)
        before = lax.ppermute(last, axis, up)
        after = lax.ppermute(initial, axis, down)
        array = jnp.concatenate([before, array, after], axis=dim)
    return array


def entering(part, axis, combine, identity, reverse):
    count = lax.axis_size(axis)
    place = lax.axis_index(axis)
    ahead = count - 1 - place if reverse else place
    gathered = jax.tree.map(lambda a: lax.all_gather(a, axis), part)
    state = jax.tree.map(lambda a, e: jnp.zeros_like(a) + jnp.asarray(e, a.dtype), part, identity)

    def one(turn, state):
        source = count - 1 - turn if reverse else turn
        return combine(
            state, jax.tree.map(lambda a: lax.dynamic_index_in_dim(a, source, 0, False), gathered)
        )

    return lax.fori_loop(0, ahead, one, state)


def expand(widened_output, expand_weight, width):
    total = None
    for shift_amount in range(3):
        term = jnp.einsum(
            "vjt,jc->vtc",
            widened_output[:, :, shift_amount : shift_amount + width],
            expand_weight[shift_amount],
            preferred_element_type=jnp.float32,
        )
        total = term if total is None else total + term
    return jax.nn.relu(total).astype(jnp.bfloat16)


def dilate(padded_input, hidden_start0, weight_rows):
    count_of_frames = hidden_start0.shape[1]
    total = None
    for shift_amount in range(3):
        term = jnp.einsum(
            "vti,ni->vtn",
            padded_input[
                :, shift_amount * DILATION_STEP : shift_amount * DILATION_STEP + count_of_frames
            ],
            weight_rows[:, shift_amount],
            preferred_element_type=jnp.float32,
        )
        total = term if total is None else total + term
    residual = hidden_start0.astype(jnp.float32)
    return (residual + jax.nn.relu(total)).astype(jnp.bfloat16)


def chain(earlier, latter):
    return (earlier[0] * latter[0], latter[0] * earlier[1] + latter[1])


def body(keypoints, visibility, expand_weight, dilated_tap_weight, join_weight, decay_rates):
    view_count = keypoints.shape[0]
    count_of_frames = keypoints.shape[2]
    coords = ((keypoints.astype(jnp.float32) - 2048.0) / 2048.0).astype(jnp.bfloat16)
    widened_output = with_halo(coords, (("tm", 2),), 1)
    hidden_start0 = expand(widened_output, expand_weight, count_of_frames)
    padded_input = with_halo(hidden_start0, (("tm", 1),), DILATION_STEP)
    hidden1 = dilate(
        padded_input, hidden_start0, lax.all_gather(dilated_tap_weight, "tm", axis=0, tiled=True)
    )
    own_mask = lax.dynamic_slice_in_dim(
        visibility, lax.axis_index("cam") * view_count, view_count, 0
    )
    masked = hidden1 * own_mask[:, :, None].astype(jnp.bfloat16)
    state_rows = decay_rates.shape[0]
    total = lax.psum_scatter(
        jnp.einsum("vti,is->st", masked, join_weight, preferred_element_type=jnp.float32).astype(
            jnp.bfloat16
        ),
        "cam",
        scatter_dimension=0,
        tiled=True,
    ).astype(jnp.float32)
    seen = jnp.sum(visibility.astype(jnp.float32), axis=0)
    joined = total / jnp.maximum(seen, 1.0)[None, :]
    decay = jnp.exp(-decay_rates)
    energy = -jnp.expm1(-2.0 * decay_rates)
    drive = jnp.sqrt(energy)
    prod_fwd, local_fwd = lax.associative_scan(chain, (decay, drive * joined), axis=1)
    ones_vec = jnp.ones((state_rows,), jnp.float32)
    zeros_vec = jnp.zeros((state_rows,), jnp.float32)
    carried = entering(
        (prod_fwd[:, -1], local_fwd[:, -1]), "tm", chain, (ones_vec, zeros_vec), False
    )
    filtered = local_fwd + prod_fwd * carried[1][:, None]
    prod_back, local_back = lax.associative_scan(
        chain, (decay, energy * filtered), axis=1, reverse=True
    )
    returned = entering(
        (prod_back[:, 0], local_back[:, 0]), "tm", chain, (ones_vec, zeros_vec), True
    )
    smoothed = local_back + prod_back * returned[1][:, None]
    return smoothed

LANES = 128
DEPTH = 72
SLOT = 8
RADIX = 4


def neg_expm1(u):
    series = jnp.ones_like(u)
    for k in range(11, 1, -1):
        series = 1.0 - series * u * (1.0 / k)
    return jnp.where(u < 0.5, u * series, 1.0 - jnp.exp(-u))


def block_kernel(
    layers, keys_hbm, vis_hbm, raw_hbm, taps_hbm, join_hbm, rates_hbm, out_ref,
    keys_ref, vis_ref, raw_ref, join_ref, rates_ref, load,
    stage, coords, edge_out, edge_in, rims, turned_rims, first_wide, first, weights, hidden, slab_hidden, slab_mixed,
    lifted, masks, joiner, powers, kept_forms, part_out, part_in, ends,
    edge_send, edge_recv, body_send, body_recv,
    mate_send, mate_recv, x_send, x_recv, y_send, y_recv, pass_send, pass_recv,
    part_send, part_recv, end_send, end_recv,
):
    joints, views, length = keys_ref.shape
    channels = raw_ref.shape[2]
    rows = taps_hbm.shape[1]
    states = rates_ref.shape[0]
    cams = 2
    group = 4
    count = layers * group
    pair = 2 * rows
    wide = length + LANES
    f32, bf16 = jnp.float32, jnp.bfloat16
    y = lax.axis_index("cam")
    i = lax.axis_index("tm")
    z = i // group
    l = i % group
    x = l // 2
    c = l % 2
    mate = z * group + 2 * x + 1 - c
    across = z * group + 2 * (1 - x) + c
    columns = (2 * x + 1 - c, 2 * (1 - x) + 1 - c)
    bent = x == c
    step = jnp.where(bent, jnp.where(c == 0, -1, 1), 0)
    spans = (i > 0) & (i < count - 1)

    barrier = pltpu.get_barrier_semaphore()

    def greet(cam, tm):
        pl.semaphore_signal(barrier, inc=1, device_id=(cam, tm), device_id_type=MESH)

    for d in range(1, count):
        greet(y, lax.rem(i + d, count))
    for d in range(layers):
        greet(1 - y, d * group + l)

    own_taps = weights.at[x, :, pl.ds(pl.multiple_of(c * rows, rows), rows), :]
    loads = [
        pltpu.make_async_copy(src, dst, load.at[n])
        for n, (src, dst) in enumerate(
            (
                (keys_hbm, keys_ref), (vis_hbm, vis_ref), (taps_hbm, own_taps),
                (raw_hbm, raw_ref), (rates_hbm, rates_ref), (join_hbm, join_ref),
            )
        )
    ]
    for copy in loads:
        copy.start()
    stage[...] = jnp.zeros_like(stage)
    loads[0].wait()
    loads[1].wait()
    for v in range(views):
        stage[pl.ds(v * joints, joints), :] = (keys_ref[:, v, :].astype(f32) - 2048.0) / 2048.0
        stage[pl.ds(views * joints + v, 1), :] = vis_ref[pl.ds(y * views + v, 1), :].astype(f32)
    coords[z] = stage[...].astype(bf16)
    rim = jnp.concatenate([stage[:, length - LANES : length], stage[:, 0:LANES]], axis=1)
    rim = jnp.concatenate([rim, jnp.zeros((LANES - DEPTH, 2 * LANES), f32)], axis=0)
    edge_out[...] = rim.T[LANES - 8 : LANES + 8].astype(bf16)
    edge_in[2, z] = edge_out[...]

    @pl.when(bent)
    def _():
        edge_in[1, jnp.where(c == 0, layers - 1, 0)] = jnp.zeros((16, LANES), bf16)

    loads[2].wait()
    pl.semaphore_wait(barrier, count - 1 + layers)

    def remote(src, dst, send_sem, recv_sem, cam, tm):
        return pltpu.make_async_remote_copy(
            src_ref=src, dst_ref=dst, send_sem=send_sem, recv_sem=recv_sem,
            device_id=(cam, tm), device_id_type=MESH,
        )

    def edge_copy(column, origin, target, n):
        return remote(
            edge_out, edge_in.at[column, origin], edge_send.at[n],
            edge_recv.at[column * layers + origin], y, target,
        )

    def edge_sends(act):
        for d in range(layers):
            act(edge_copy(0, z, d * group + columns[0], d))
            if d > 0:
                peer = lax.rem(z + d, layers)
                act(edge_copy(2, z, peer * group + l, 2 * layers + d))

            @pl.when(spans)
            def _():
                act(edge_copy(1, z, d * group + columns[1], layers + d))

    def body_copy(origin, target):
        return remote(
            coords.at[origin], coords.at[origin], body_send.at[target], body_recv.at[origin],
            y, target * group + l,
        )

    def source(k):
        if k == 0:
            return z
        if k == 1:
            return jnp.where(z < layers - 1, z + 1, z - 1)
        if k == 2:
            return jnp.where(z == 0, 2, z - 1 - jnp.where(z == layers - 1, 1, 0))
        return jnp.where(z < 2, 3, 0)

    sources = [source(k) for k in range(layers)]

    quarter = rows // 4
    x_parts = ((y, 0, 2), (y, 2, 1), (y, 3, 1), (2, 0, 4), (1 - y, 3, 1))
    y_parts = ((1 - y, 0, 2), (1 - y, 2, 1))

    def block(ref, part, base):
        o, start, size = part
        return ref.at[o, pl.ds(pl.multiple_of(base + start * quarter, quarter), size * quarter), :]

    def mate_copy(cs):
        at = weights.at[x, :, pl.ds(pl.multiple_of(cs * rows, rows), rows), :]
        return remote(at, at, mate_send, mate_recv, y, mate)

    def x_copy(n, first):
        at = block(weights.at[x if first else 1 - x], x_parts[n], c * rows)
        return remote(at, at, x_send.at[n], x_recv.at[n], y, across)

    def y_copy(n, first):
        part = x_parts[n] if first else y_parts[n]
        at = block(weights.at[1 - x], part, c * rows)
        return remote(at, at, y_send.at[n], y_recv.at[n], 1 - y, i)

    def pass_copy(n, cs):
        at = block(weights.at[1 - x], (x_parts + y_parts)[n], cs * rows)
        return remote(at, at, pass_send.at[n], pass_recv.at[n], y, mate)

    x_copy(0, True).start()
    edge_sends(lambda copy: copy.start())
    body_copy(z, sources[1]).start()
    x_copy(1, True).start()
    body_copy(z, sources[2]).start()
    mate_copy(c).start()
    for n in range(2, 5):
        x_copy(n, True).start()
    body_copy(z, sources[3]).start()

    def serve_x(n):
        x_copy(n, False).wait_recv()
        if n < 2:
            y_copy(n, True).start()
        pass_copy(n, c).start()

    def serve_y(n):
        y_copy(n, False).wait_recv()
        pass_copy(5 + n, c).start()

    loads[3].wait()
    first_wide[...] = jnp.zeros_like(first_wide)
    for o in range(3):
        first_wide[pl.ds(o * DEPTH, joints), :] = raw_ref[o].astype(f32)
    turned = first_wide[...].T
    first[0] = turned[:, : 3 * DEPTH].astype(bf16)
    first[1] = pltpu.roll(turned, joints, 1)[:, : 3 * DEPTH].astype(bf16)
    loads[5].wait()
    for n, xs in ((0, x), (1, 1 - x)):
        joiner[:, n * pair : (n + 1) * pair] = join_ref[
            :, pl.ds(pl.multiple_of(z * 2 * pair + xs * pair, pair), pair)
        ]

    rim_lane = lax.broadcasted_iota(jnp.int32, (3 * DEPTH, LANES), 1)
    body_lane = lax.broadcasted_iota(jnp.int32, (DEPTH, length), 1)
    rims[...] = jnp.zeros_like(rims)

    def gather_rim(k):
        s = sources[k]
        if k > 0:
            edge_copy(2, s, i, 0).wait_recv()
        edge_copy(0, s, i, 0).wait_recv()
        ahead = s + step
        inside = (ahead >= 0) & (ahead < layers)

        @pl.when(inside)
        def _():
            edge_copy(1, ahead, i, 0).wait_recv()

        near = edge_in[0, s].astype(f32)
        away = edge_in[1, lax.rem(ahead + layers, layers)].astype(f32)
        away = jnp.where(inside, away, 0.0)
        own = edge_in[2, s].astype(f32)
        right = jnp.where(c == 0, near, away)
        left = jnp.where(c == 0, away, near)
        rims[4 * SLOT * k : 4 * SLOT * (k + 1), :] = jnp.concatenate(
            [left[0:8], own[8:16], own[0:8], right[8:16]], axis=0
        )

    def expand_shard(k):
        if k > 0:
            body_copy(sources[k], z).wait_recv()
        rim = turned_rims[min(k, 1), 0:DEPTH, :]
        at = 4 * SLOT * k
        e = coords[sources[k]].astype(f32)
        masks[k] = e[DEPTH - 8 : DEPTH]
        before = jnp.where(body_lane == 0, rim[:, at + 7 : at + 8], pltpu.roll(e, 1, 1))
        after = jnp.where(
            body_lane == length - 1, rim[:, at + 24 : at + 25], pltpu.roll(e, length - 1, 1)
        )
        body = jnp.concatenate([before, e, after], axis=0).astype(bf16)
        for v in range(views):
            h = jnp.dot(first[v], body, preferred_element_type=f32)
            hidden[k, v] = jnp.maximum(h, 0.0).astype(bf16)

    own_rows = weights.at[x]
    other_rows = weights.at[1 - x]

    def lift(a, n, k, v, xs):
        rest = hidden[k, v, pl.ds(pl.multiple_of(z * 2 * pair + xs * pair, pair), pair), :]
        at = 4 * SLOT * k
        cols = slice(v * LANES, (v + 1) * LANES)
        older = pltpu.roll(slab_mixed[min(k, 1), n, 0:pair, cols], (2 * LANES - 8 - at) % LANES, 1)
        newer = pltpu.roll(slab_mixed[min(k, 1), n, 2 * pair :, cols], (LANES - 24 - at) % LANES, 1)
        left = pltpu.roll(jnp.concatenate([a[0:pair], older], axis=1), DILATION_STEP, 1)
        right = pltpu.roll(
            jnp.concatenate([a[2 * pair :], newer], axis=1), wide - DILATION_STEP, 1
        )
        acc = left[:, :length] + a[pair : 2 * pair] + right[:, :length]
        return (rest.astype(f32) + jnp.maximum(acc, 0.0)).astype(bf16)

    def early(k):
        w = own_rows[...].reshape(3 * pair, channels)
        for v in range(views):
            a = jnp.dot(w, hidden[k, v], preferred_element_type=f32)
            lifted[k, v, 0:pair] = lift(a, 0, k, v, x)

    def late(k, v):
        w = other_rows[...].reshape(3 * pair, channels)
        b = jnp.dot(w, hidden[k, v], preferred_element_type=f32)
        lifted[k, v, pair : 2 * pair] = lift(b, 1, k, v, 1 - x)

    def weighed(k, v):
        at = views * joints % 8 + v
        return masks[k, at : at + 1, :] * jnp.dot(
            joiner[...], lifted[k, v], preferred_element_type=f32
        )

    def join(k, total=0.0, done=0):
        for v in range(done, views):
            total = total + weighed(k, v)
        for cam in range(cams):
            part_out[k, cam] = total[cam * states : (cam + 1) * states].astype(bf16)

    def give(k):
        if k > 0:
            for cam in range(cams):
                part_copy(k, cam, sources[k] * group + l).start()
        else:
            part_copy(0, 1 - y, i).start()
            part_in[z * cams + y] = part_out[0, y]

    def part_copy(k, cam, tm):
        return remote(
            part_out.at[k, cam], part_in.at[z * cams + y], part_send.at[k * cams + cam],
            part_recv.at[z * cams + y], cam, tm,
        )

    lane = lax.broadcasted_iota(jnp.int32, (states, length), 1)

    levels = []
    base = 1
    while base < length:
        levels.append([n * base for n in range(1, RADIX) if n * base < length])
        base *= RADIX

    def place(shift, reverse):
        turn = length - shift if reverse else shift
        return turn, (lane < length - shift) if reverse else (lane >= shift)

    def products(prod, reverse):
        at = int(reverse) * sum(map(len, levels))
        for shifts in levels:
            unit = prod
            for shift in shifts:
                turn, fits = place(shift, reverse)
                powers[at] = jnp.where(fits, prod, 0.0)
                at += 1
                prod = prod * jnp.where(fits, pltpu.roll(unit, turn, 1), 1.0)
        return prod

    def scan(value, reverse):
        at = int(reverse) * sum(map(len, levels))
        for shifts in levels:
            terms = [value]
            for shift in shifts:
                turn, _ = place(shift, reverse)
                terms.append(powers[at] * pltpu.roll(value, turn, 1))
                at += 1
            while len(terms) > 1:
                terms = [sum(terms[n : n + 2][1:], terms[n]) for n in range(0, len(terms), 2)]
            value = terms[0]
        return value

    loads[4].wait()
    rates = rates_ref[...]
    decay = jnp.exp(-rates)
    energy = neg_expm1(2.0 * rates)
    kept_forms[0] = products(decay, False)
    kept_forms[1] = products(decay, True)
    kept_forms[2] = scan(energy * kept_forms[0], True)
    kept_forms[3] = energy
    seen = jnp.sum(vis_ref[...].astype(f32), axis=0, keepdims=True)
    kept_forms[4] = jnp.sqrt(energy) / jnp.maximum(seen, 1.0)

    def slab(part):
        members = range(1) if part == 0 else range(1, layers)
        for k in members:
            gather_rim(k)
        rim = rims[...].T
        turned_rims[part] = rim
        rim = rim[0:DEPTH, :]
        tile = jnp.concatenate([pltpu.roll(rim, 1, 1), rim, pltpu.roll(rim, LANES - 1, 1)], axis=0)
        for k in members:
            shard = sources[k] * group + l
            at = 4 * SLOT * k
            begins = (shard == 0) & (rim_lane >= at) & (rim_lane < at + 8)
            ends_here = (shard == count - 1) & (rim_lane >= at + 24) & (rim_lane < at + 32)
            tile = jnp.where(begins | ends_here, 0.0, tile)
        tile = tile.astype(bf16)
        for v in range(views):
            h = jnp.dot(first[v], tile, preferred_element_type=f32)
            slab_hidden[part, :, v * LANES : (v + 1) * LANES] = jnp.maximum(h, 0.0).astype(bf16)

    def slab_mix(part, n):
        w = (other_rows if n else own_rows)[...].reshape(3 * pair, channels)
        slab_mixed[part, n] = jnp.dot(w, slab_hidden[part], preferred_element_type=f32)

    slab(0)
    expand_shard(0)
    serve_x(0)
    mate_copy(1 - c).wait_recv()
    slab_mix(0, 0)
    serve_x(1)
    early(0)
    serve_x(2)
    slab(1)
    slab_mix(1, 0)
    expand_shard(1)
    early(1)
    serve_x(3)
    serve_y(0)
    serve_x(4)
    serve_y(1)
    expand_shard(2)
    early(2)
    expand_shard(3)
    early(3)
    for n in range(7):
        pass_copy(n, 1 - c).wait_recv()
    slab_mix(0, 1)
    slab_mix(1, 1)
    for k in range(layers - 1, -1, -1):
        late(k, 0)
        if k < layers - 1:
            join(k + 1)
            give(k + 1)
        begun = weighed(0, 0) if k == 0 else 0.0
        late(k, 1)
    join(0, begun, 1)
    give(0)

    members = cams * layers
    me = z * cams + y
    for d in range(1, members):
        other = lax.rem(me + d, members)
        remote(
            part_in.at[other], part_in.at[other], part_send.at[0], part_recv.at[other],
            other % cams, (other // cams) * group + l,
        ).wait_recv()
    summed = part_in[0].astype(f32)
    for p in range(1, members):
        summed = summed + part_in[p].astype(f32)
    local = scan(kept_forms[4] * summed, False)
    back = scan(kept_forms[3] * local, True)
    prod_fwd, prod_back, through = kept_forms[0], kept_forms[1], kept_forms[2]

    square = lax.broadcasted_iota(jnp.int32, (states, LANES), 1)
    packed = jnp.where(
        square == 0,
        prod_fwd[:, length - 1 : length],
        jnp.where(
            square == 1,
            local[:, length - 1 : length],
            jnp.where(square == 2, back[:, 0:1], through[:, 0:1]),
        ),
    )
    packed = jnp.concatenate([packed, jnp.zeros((LANES - states, LANES), f32)], axis=0)
    ends[i] = packed.T[0:8]

    def end_copy(origin, target, sem):
        return remote(ends.at[origin], ends.at[origin], sem, end_recv.at[origin], y, target)

    for k in range(layers - 1, -1, -1):
        for d in range(group):
            if k + d > 0:
                target = sources[k] * group + lax.rem(l + d, group)
                end_copy(i, target, end_send.at[target]).start()
    for d in range(1, count):
        origin = lax.rem(i + count - d, count)
        end_copy(origin, origin, end_send.at[origin]).wait_recv()

    entry = jnp.zeros((1, LANES), f32)
    carried = entry
    entries = []
    for j in range(count):
        entries.append(entry)
        carried = jnp.where(j == i, entry, carried)
        entry = ends[j, 0:1] * entry + ends[j, 1:2]
    state = jnp.zeros((1, LANES), f32)
    returned = state
    for j in range(count - 1, -1, -1):
        returned = jnp.where(j == i, state, returned)
        state = ends[j, 0:1] * state + ends[j, 2:3] + ends[j, 3:4] * entries[j]
    both = jnp.concatenate([carried, returned, jnp.zeros((LANES - 2, LANES), f32)], axis=0).T
    out_ref[...] = back + through * both[0:states, 0:1] + prod_back * both[0:states, 1:2]

    edge_sends(lambda copy: copy.wait_send())
    for k in range(1, layers):
        body_copy(z, sources[k]).wait_send()
    mate_copy(c).wait_send()
    for n in range(5):
        x_copy(n, True).wait_send()
    for n in range(2):
        y_copy(n, True).wait_send()
    for n in range(7):
        pass_copy(n, c).wait_send()

    for k in range(1, layers):
        for cam in range(cams):
            part_copy(k, cam, sources[k] * group + l).wait_send()
    part_copy(0, 1 - y, i).wait_send()
    for d in range(1, count):
        target = lax.rem(i + d, count)
        end_copy(i, target, end_send.at[target]).wait_send()


def block_body(cams, count, group):
    layers = count // group

    def run(keypoints, visibility, expand_weight, dilated_tap_weight, join_weight, decay_rates):
        views, joints, length = keypoints.shape
        channels = expand_weight.shape[2]
        rows = dilated_tap_weight.shape[0]
        states = decay_rates.shape[0]
        keys = jnp.transpose(keypoints, (1, 0, 2))
        taps = jnp.transpose(dilated_tap_weight, (1, 0, 2))
        wide = length + LANES
        steps = 0
        base = 1
        while base < length:
            steps += sum(n * base < length for n in range(1, RADIX))
            base *= RADIX
        dma, vmem = (pltpu.SemaphoreType.DMA, pltpu.VMEM)
        f32, bf16 = jnp.float32, jnp.bfloat16
        sems = [3 * layers] * 2 + [layers] * 2 + [0] * 2 + [5, 5, 2, 2, 7, 7] + [cams * layers] * 2 + [count] * 2
        return pl.pallas_call(
            functools.partial(block_kernel, layers),
            out_shape=jax.ShapeDtypeStruct(decay_rates.shape, f32),
            in_specs=[pl.BlockSpec(memory_space=pl.ANY)] * 6,
            out_specs=pl.BlockSpec(memory_space=pltpu.VMEM),
            scratch_shapes=[
                vmem(keys.shape, jnp.int32),
                vmem(visibility.shape, jnp.int32),
                vmem(expand_weight.shape, bf16),
                vmem((states * cams, channels), bf16),
                vmem(decay_rates.shape, f32),
                dma((6,)),
                vmem((DEPTH, length), f32),
                vmem((layers, DEPTH, length), bf16),
                vmem((16, LANES), bf16),
                vmem((3, layers, 16, LANES), bf16),
                vmem((LANES, LANES), f32),
                vmem((2, LANES, LANES), f32),
                vmem((2 * LANES, channels), f32),
                vmem((views, channels, 3 * DEPTH), bf16),
                vmem((2, 3, 2 * rows, channels), bf16),
                vmem((layers, views, channels, length), bf16),
                vmem((2, channels, views * LANES), bf16),
                vmem((2, 2, 6 * rows, views * LANES), f32),
                vmem((layers, views, 4 * rows, length), bf16),
                vmem((layers, 8, length), f32),
                vmem((cams * states, 4 * rows), bf16),
                vmem((2 * steps, states, length), f32),
                vmem((5, states, length), f32),
                vmem((layers, cams, states, length), bf16),
                vmem((cams * layers, states, length), bf16),
                vmem((count, 8, LANES), f32),
            ]
            + [dma((n,)) if n else dma for n in sems],
            compiler_params=pltpu.CompilerParams(
                collective_id=0, has_side_effects=True, vmem_limit_bytes=58 * 1024 * 1024
            ),
        )(keys, visibility, expand_weight, taps, join_weight.T, decay_rates)

    return run


def solution(mesh):
    cams, count = mesh.shape["cam"], mesh.shape["tm"]
    group = 4
    fits = count % group == 0 and cams == 2 and count == 4 * group
    return jax.shard_map(
        block_body(cams, count, group) if fits else body,
        mesh=mesh,
        in_specs=(
            P("cam", None, "tm"),
            P(None, "tm"),
            P(),
            P("tm", None, None),
            P(),
            P("cam", "tm"),
        ),
        out_specs=P("cam", "tm"),
        check_vma=False,
    )
```

```python
import functools

import jax
import jax.numpy as jnp
from jax import lax
from jax.experimental import pallas as pl
from jax.experimental.pallas import tpu as pltpu
from jax.sharding import PartitionSpec as P

DILATION_STEP = 3
MESH = pl.DeviceIdType.MESH


def with_halo(array, sides, width):
    for axis, dim in sides:
        count, length = (lax.axis_size(axis), array.shape[dim])
        up = [(i, (i + 1) % count) for i in range(count - 1)]
        down = [(j, i) for i, j in up]
        last = lax.slice_in_dim(array, length - width, length, axis=dim)
        initial = lax.slice_in_dim(array, 0, width, axis=dim)
        before = lax.ppermute(last, axis, up)
        after = lax.ppermute(initial, axis, down)
        array = jnp.concatenate([before, array, after], axis=dim)
    return array


def entering(part, axis, combine, identity, reverse):
    count = lax.axis_size(axis)
    place = lax.axis_index(axis)
    ahead = count - 1 - place if reverse else place
    gathered = jax.tree.map(lambda a: lax.all_gather(a, axis), part)
    state = jax.tree.map(lambda a, e: jnp.zeros_like(a) + jnp.asarray(e, a.dtype), part, identity)

    def one(turn, state):
        source = count - 1 - turn if reverse else turn
        return combine(
            state, jax.tree.map(lambda a: lax.dynamic_index_in_dim(a, source, 0, False), gathered)
        )

    return lax.fori_loop(0, ahead, one, state)


def expand(widened_output, expand_weight, width):
    total = None
    for shift_amount in range(3):
        term = jnp.einsum(
            "vjt,jc->vtc",
            widened_output[:, :, shift_amount : shift_amount + width],
            expand_weight[shift_amount],
            preferred_element_type=jnp.float32,
        )
        total = term if total is None else total + term
    return jax.nn.relu(total).astype(jnp.bfloat16)


def dilate(padded_input, hidden_start0, weight_rows):
    count_of_frames = hidden_start0.shape[1]
    total = None
    for shift_amount in range(3):
        term = jnp.einsum(
            "vti,ni->vtn",
            padded_input[
                :, shift_amount * DILATION_STEP : shift_amount * DILATION_STEP + count_of_frames
            ],
            weight_rows[:, shift_amount],
            preferred_element_type=jnp.float32,
        )
        total = term if total is None else total + term
    residual = hidden_start0.astype(jnp.float32)
    return (residual + jax.nn.relu(total)).astype(jnp.bfloat16)


def chain(earlier, latter):
    return (earlier[0] * latter[0], latter[0] * earlier[1] + latter[1])


def body(keypoints, visibility, expand_weight, dilated_tap_weight, join_weight, decay_rates):
    view_count = keypoints.shape[0]
    count_of_frames = keypoints.shape[2]
    coords = ((keypoints.astype(jnp.float32) - 2048.0) / 2048.0).astype(jnp.bfloat16)
    widened_output = with_halo(coords, (("tm", 2),), 1)
    hidden_start0 = expand(widened_output, expand_weight, count_of_frames)
    padded_input = with_halo(hidden_start0, (("tm", 1),), DILATION_STEP)
    hidden1 = dilate(
        padded_input, hidden_start0, lax.all_gather(dilated_tap_weight, "tm", axis=0, tiled=True)
    )
    own_mask = lax.dynamic_slice_in_dim(
        visibility, lax.axis_index("cam") * view_count, view_count, 0
    )
    masked = hidden1 * own_mask[:, :, None].astype(jnp.bfloat16)
    state_rows = decay_rates.shape[0]
    total = lax.psum_scatter(
        jnp.einsum("vti,is->st", masked, join_weight, preferred_element_type=jnp.float32).astype(
            jnp.bfloat16
        ),
        "cam",
        scatter_dimension=0,
        tiled=True,
    ).astype(jnp.float32)
    seen = jnp.sum(visibility.astype(jnp.float32), axis=0)
    joined = total / jnp.maximum(seen, 1.0)[None, :]
    decay = jnp.exp(-decay_rates)
    energy = -jnp.expm1(-2.0 * decay_rates)
    drive = jnp.sqrt(energy)
    prod_fwd, local_fwd = lax.associative_scan(chain, (decay, drive * joined), axis=1)
    ones_vec = jnp.ones((state_rows,), jnp.float32)
    zeros_vec = jnp.zeros((state_rows,), jnp.float32)
    carried = entering(
        (prod_fwd[:, -1], local_fwd[:, -1]), "tm", chain, (ones_vec, zeros_vec), False
    )
    filtered = local_fwd + prod_fwd * carried[1][:, None]
    prod_back, local_back = lax.associative_scan(
        chain, (decay, energy * filtered), axis=1, reverse=True
    )
    returned = entering(
        (prod_back[:, 0], local_back[:, 0]), "tm", chain, (ones_vec, zeros_vec), True
    )
    smoothed = local_back + prod_back * returned[1][:, None]
    return smoothed

LANES = 128
DEPTH = 72
SLOT = 8
RADIX = 4


def neg_expm1(u):
    series = jnp.ones_like(u)
    for k in range(11, 1, -1):
        series = 1.0 - series * u * (1.0 / k)
    return jnp.where(u < 0.5, u * series, 1.0 - jnp.exp(-u))


def block_kernel(
    layers, keys_hbm, vis_hbm, raw_hbm, taps_hbm, join_hbm, rates_hbm, out_ref,
    keys_ref, vis_ref, raw_ref, join_ref, rates_ref, load,
    stage, coords, edge_out, edge_in, rims, turned_rims, first_wide, first, weights, hidden, slab_hidden, slab_mixed,
    lifted, masks, joiner, powers, kept_forms, part_out, part_in, ends,
    edge_send, edge_recv, body_send, body_recv,
    mate_send, mate_recv, x_send, x_recv, y_send, y_recv, pass_send, pass_recv,
    part_send, part_recv, end_send, end_recv,
):
    joints, views, length = keys_ref.shape
    channels = raw_ref.shape[2]
    rows = taps_hbm.shape[1]
    states = rates_ref.shape[0]
    cams = 2
    group = 4
    count = layers * group
    pair = 2 * rows
    wide = length + LANES
    f32, bf16 = jnp.float32, jnp.bfloat16
    y = lax.axis_index("cam")
    i = lax.axis_index("tm")
    z = i // group
    l = i % group
    x = l // 2
    c = l % 2
    mate = z * group + 2 * x + 1 - c
    across = z * group + 2 * (1 - x) + c
    columns = (2 * x + 1 - c, 2 * (1 - x) + 1 - c)
    bent = x == c
    step = jnp.where(bent, jnp.where(c == 0, -1, 1), 0)
    spans = (i > 0) & (i < count - 1)

    barrier = pltpu.get_barrier_semaphore()

    def greet(cam, tm):
        pl.semaphore_signal(barrier, inc=1, device_id=(cam, tm), device_id_type=MESH)

    for d in range(1, count):
        greet(y, lax.rem(i + d, count))
    for d in range(layers):
        greet(1 - y, d * group + l)

    own_taps = weights.at[x, :, pl.ds(pl.multiple_of(c * rows, rows), rows), :]
    loads = [
        pltpu.make_async_copy(src, dst, load.at[n])
        for n, (src, dst) in enumerate(
            (
                (keys_hbm, keys_ref), (vis_hbm, vis_ref), (taps_hbm, own_taps),
                (raw_hbm, raw_ref), (rates_hbm, rates_ref), (join_hbm, join_ref),
            )
        )
    ]
    for copy in loads:
        copy.start()
    stage[...] = jnp.zeros_like(stage)
    loads[0].wait()
    loads[1].wait()
    for v in range(views):
        stage[pl.ds(v * joints, joints), :] = (keys_ref[:, v, :].astype(f32) - 2048.0) / 2048.0
        stage[pl.ds(views * joints + v, 1), :] = vis_ref[pl.ds(y * views + v, 1), :].astype(f32)
    coords[z] = stage[...].astype(bf16)
    rim = jnp.concatenate([stage[:, length - LANES : length], stage[:, 0:LANES]], axis=1)
    rim = jnp.concatenate([rim, jnp.zeros((LANES - DEPTH, 2 * LANES), f32)], axis=0)
    edge_out[...] = rim.T[LANES - 8 : LANES + 8].astype(bf16)
    edge_in[2, z] = edge_out[...]

    @pl.when(bent)
    def _():
        edge_in[1, jnp.where(c == 0, layers - 1, 0)] = jnp.zeros((16, LANES), bf16)

    loads[2].wait()
    pl.semaphore_wait(barrier, count - 1 + layers)

    def remote(src, dst, send_sem, recv_sem, cam, tm):
        return pltpu.make_async_remote_copy(
            src_ref=src, dst_ref=dst, send_sem=send_sem, recv_sem=recv_sem,
            device_id=(cam, tm), device_id_type=MESH,
        )

    def edge_copy(column, origin, target, n):
        return remote(
            edge_out, edge_in.at[column, origin], edge_send.at[n],
            edge_recv.at[column * layers + origin], y, target,
        )

    def edge_sends(act):
        for d in range(layers):
            act(edge_copy(0, z, d * group + columns[0], d))
            if d > 0:
                peer = lax.rem(z + d, layers)
                act(edge_copy(2, z, peer * group + l, 2 * layers + d))

            @pl.when(spans)
            def _():
                act(edge_copy(1, z, d * group + columns[1], layers + d))

    def body_copy(origin, target):
        return remote(
            coords.at[origin], coords.at[origin], body_send.at[target], body_recv.at[origin],
            y, target * group + l,
        )

    def source(k):
        if k == 0:
            return z
        if k == 1:
            return jnp.where(z < layers - 1, z + 1, z - 1)
        if k == 2:
            return jnp.where(z == 0, 2, z - 1 - jnp.where(z == layers - 1, 1, 0))
        return jnp.where(z < 2, 3, 0)

    sources = [source(k) for k in range(layers)]

    quarter = rows // 4
    x_parts = ((y, 0, 2), (y, 2, 2), (2, 0, 4))
    y_parts = ((1 - y, 0, 2), (1 - y, 2, 2))

    def block(ref, part, base):
        o, start, size = part
        return ref.at[o, pl.ds(pl.multiple_of(base + start * quarter, quarter), size * quarter), :]

    def mate_copy(cs):
        at = weights.at[x, :, pl.ds(pl.multiple_of(cs * rows, rows), rows), :]
        return remote(at, at, mate_send, mate_recv, y, mate)

    def x_copy(n, first):
        at = block(weights.at[x if first else 1 - x], x_parts[n], c * rows)
        return remote(at, at, x_send.at[n], x_recv.at[n], y, across)

    def y_copy(n, first):
        part = x_parts[n] if first else y_parts[n]
        at = block(weights.at[1 - x], part, c * rows)
        return remote(at, at, y_send.at[n], y_recv.at[n], 1 - y, i)

    def pass_copy(n, cs):
        at = block(weights.at[1 - x], (x_parts + y_parts)[n], cs * rows)
        return remote(at, at, pass_send.at[n], pass_recv.at[n], y, mate)

    x_copy(0, True).start()
    edge_sends(lambda copy: copy.start())
    body_copy(z, sources[1]).start()
    x_copy(1, True).start()
    body_copy(z, sources[2]).start()
    mate_copy(c).start()
    x_copy(2, True).start()
    body_copy(z, sources[3]).start()

    def serve_x(n):
        x_copy(n, False).wait_recv()
        if n < 2:
            y_copy(n, True).start()
        pass_copy(n, c).start()

    def serve_y(n):
        y_copy(n, False).wait_recv()
        pass_copy(3 + n, c).start()

    loads[3].wait()
    first_wide[...] = jnp.zeros_like(first_wide)
    for o in range(3):
        first_wide[pl.ds(o * DEPTH, joints), :] = raw_ref[o].astype(f32)
    turned = first_wide[...].T
    first[0] = turned[:, : 3 * DEPTH].astype(bf16)
    first[1] = pltpu.roll(turned, joints, 1)[:, : 3 * DEPTH].astype(bf16)
    loads[5].wait()
    for n, xs in ((0, x), (1, 1 - x)):
        joiner[:, n * pair : (n + 1) * pair] = join_ref[
            :, pl.ds(pl.multiple_of(z * 2 * pair + xs * pair, pair), pair)
        ]

    rim_lane = lax.broadcasted_iota(jnp.int32, (3 * DEPTH, LANES), 1)
    body_lane = lax.broadcasted_iota(jnp.int32, (DEPTH, length), 1)
    rims[...] = jnp.zeros_like(rims)

    def gather_rim(k):
        s = sources[k]
        if k > 0:
            edge_copy(2, s, i, 0).wait_recv()
        edge_copy(0, s, i, 0).wait_recv()
        ahead = s + step
        inside = (ahead >= 0) & (ahead < layers)

        @pl.when(inside)
        def _():
            edge_copy(1, ahead, i, 0).wait_recv()

        near = edge_in[0, s].astype(f32)
        away = edge_in[1, lax.rem(ahead + layers, layers)].astype(f32)
        away = jnp.where(inside, away, 0.0)
        own = edge_in[2, s].astype(f32)
        right = jnp.where(c == 0, near, away)
        left = jnp.where(c == 0, away, near)
        rims[4 * SLOT * k : 4 * SLOT * (k + 1), :] = jnp.concatenate(
            [left[0:8], own[8:16], own[0:8], right[8:16]], axis=0
        )

    def expand_shard(k):
        if k > 0:
            body_copy(sources[k], z).wait_recv()
        rim = turned_rims[min(k, 1), 0:DEPTH, :]
        at = 4 * SLOT * k
        e = coords[sources[k]].astype(f32)
        masks[k] = e[DEPTH - 8 : DEPTH]
        before = jnp.where(body_lane == 0, rim[:, at + 7 : at + 8], pltpu.roll(e, 1, 1))
        after = jnp.where(
            body_lane == length - 1, rim[:, at + 24 : at + 25], pltpu.roll(e, length - 1, 1)
        )
        body = jnp.concatenate([before, e, after], axis=0).astype(bf16)
        for v in range(views):
            h = jnp.dot(first[v], body, preferred_element_type=f32)
            hidden[k, v] = jnp.maximum(h, 0.0).astype(bf16)

    own_rows = weights.at[x]
    other_rows = weights.at[1 - x]

    def lift(a, n, k, v, xs):
        rest = hidden[k, v, pl.ds(pl.multiple_of(z * 2 * pair + xs * pair, pair), pair), :]
        at = 4 * SLOT * k
        cols = slice(v * LANES, (v + 1) * LANES)
        older = pltpu.roll(slab_mixed[min(k, 1), n, 0:pair, cols], (2 * LANES - 8 - at) % LANES, 1)
        newer = pltpu.roll(slab_mixed[min(k, 1), n, 2 * pair :, cols], (LANES - 24 - at) % LANES, 1)
        left = pltpu.roll(jnp.concatenate([a[0:pair], older], axis=1), DILATION_STEP, 1)
        right = pltpu.roll(
            jnp.concatenate([a[2 * pair :], newer], axis=1), wide - DILATION_STEP, 1
        )
        acc = left[:, :length] + a[pair : 2 * pair] + right[:, :length]
        return (rest.astype(f32) + jnp.maximum(acc, 0.0)).astype(bf16)

    def early(k):
        w = own_rows[...].reshape(3 * pair, channels)
        for v in range(views):
            a = jnp.dot(w, hidden[k, v], preferred_element_type=f32)
            lifted[k, v, 0:pair] = lift(a, 0, k, v, x)

    def late(k, v):
        w = other_rows[...].reshape(3 * pair, channels)
        b = jnp.dot(w, hidden[k, v], preferred_element_type=f32)
        lifted[k, v, pair : 2 * pair] = lift(b, 1, k, v, 1 - x)

    def weighed(k, v):
        at = views * joints % 8 + v
        return masks[k, at : at + 1, :] * jnp.dot(
            joiner[...], lifted[k, v], preferred_element_type=f32
        )

    def join(k, total=0.0, done=0):
        for v in range(done, views):
            total = total + weighed(k, v)
        for cam in range(cams):
            part_out[k, cam] = total[cam * states : (cam + 1) * states].astype(bf16)

    def give(k):
        if k > 0:
            for cam in range(cams):
                part_copy(k, cam, sources[k] * group + l).start()
        else:
            part_copy(0, 1 - y, i).start()
            part_in[z * cams + y] = part_out[0, y]

    def part_copy(k, cam, tm):
        return remote(
            part_out.at[k, cam], part_in.at[z * cams + y], part_send.at[k * cams + cam],
            part_recv.at[z * cams + y], cam, tm,
        )

    lane = lax.broadcasted_iota(jnp.int32, (states, length), 1)

    levels = []
    base = 1
    while base < length:
        levels.append([n * base for n in range(1, RADIX) if n * base < length])
        base *= RADIX

    def place(shift, reverse):
        turn = length - shift if reverse else shift
        return turn, (lane < length - shift) if reverse else (lane >= shift)

    def products(prod, reverse):
        at = int(reverse) * sum(map(len, levels))
        for shifts in levels:
            unit = prod
            for shift in shifts:
                turn, fits = place(shift, reverse)
                powers[at] = jnp.where(fits, prod, 0.0)
                at += 1
                prod = prod * jnp.where(fits, pltpu.roll(unit, turn, 1), 1.0)
        return prod

    def scan(value, reverse):
        at = int(reverse) * sum(map(len, levels))
        for shifts in levels:
            terms = [value]
            for shift in shifts:
                turn, _ = place(shift, reverse)
                terms.append(powers[at] * pltpu.roll(value, turn, 1))
                at += 1
            while len(terms) > 1:
                terms = [sum(terms[n : n + 2][1:], terms[n]) for n in range(0, len(terms), 2)]
            value = terms[0]
        return value

    loads[4].wait()
    rates = rates_ref[...]
    decay = jnp.exp(-rates)
    energy = neg_expm1(2.0 * rates)
    kept_forms[0] = products(decay, False)
    kept_forms[1] = products(decay, True)
    kept_forms[2] = scan(energy * kept_forms[0], True)
    kept_forms[3] = energy
    seen = jnp.sum(vis_ref[...].astype(f32), axis=0, keepdims=True)
    kept_forms[4] = jnp.sqrt(energy) / jnp.maximum(seen, 1.0)

    def slab(part):
        members = range(1) if part == 0 else range(1, layers)
        for k in members:
            gather_rim(k)
        rim = rims[...].T
        turned_rims[part] = rim
        rim = rim[0:DEPTH, :]
        tile = jnp.concatenate([pltpu.roll(rim, 1, 1), rim, pltpu.roll(rim, LANES - 1, 1)], axis=0)
        for k in members:
            shard = sources[k] * group + l
            at = 4 * SLOT * k
            begins = (shard == 0) & (rim_lane >= at) & (rim_lane < at + 8)
            ends_here = (shard == count - 1) & (rim_lane >= at + 24) & (rim_lane < at + 32)
            tile = jnp.where(begins | ends_here, 0.0, tile)
        tile = tile.astype(bf16)
        for v in range(views):
            h = jnp.dot(first[v], tile, preferred_element_type=f32)
            slab_hidden[part, :, v * LANES : (v + 1) * LANES] = jnp.maximum(h, 0.0).astype(bf16)

    def slab_mix(part, n):
        w = (other_rows if n else own_rows)[...].reshape(3 * pair, channels)
        slab_mixed[part, n] = jnp.dot(w, slab_hidden[part], preferred_element_type=f32)

    slab(0)
    expand_shard(0)
    serve_x(0)
    mate_copy(1 - c).wait_recv()
    slab_mix(0, 0)
    serve_x(1)
    early(0)
    slab(1)
    slab_mix(1, 0)
    expand_shard(1)
    early(1)
    serve_x(2)
    serve_y(0)
    serve_y(1)
    expand_shard(2)
    early(2)
    expand_shard(3)
    early(3)
    for n in range(5):
        pass_copy(n, 1 - c).wait_recv()
    slab_mix(0, 1)
    slab_mix(1, 1)
    for k in range(layers - 1, -1, -1):
        late(k, 0)
        if k < layers - 1:
            join(k + 1)
            give(k + 1)
        begun = weighed(0, 0) if k == 0 else 0.0
        late(k, 1)
    join(0, begun, 1)
    give(0)

    members = cams * layers
    me = z * cams + y
    for d in range(1, members):
        other = lax.rem(me + d, members)
        remote(
            part_in.at[other], part_in.at[other], part_send.at[0], part_recv.at[other],
            other % cams, (other // cams) * group + l,
        ).wait_recv()
    summed = part_in[0].astype(f32)
    for p in range(1, members):
        summed = summed + part_in[p].astype(f32)
    local = scan(kept_forms[4] * summed, False)
    back = scan(kept_forms[3] * local, True)
    prod_fwd, prod_back, through = kept_forms[0], kept_forms[1], kept_forms[2]

    square = lax.broadcasted_iota(jnp.int32, (states, LANES), 1)
    packed = jnp.where(
        square == 0,
        prod_fwd[:, length - 1 : length],
        jnp.where(
            square == 1,
            local[:, length - 1 : length],
            jnp.where(square == 2, back[:, 0:1], through[:, 0:1]),
        ),
    )
    packed = jnp.concatenate([packed, jnp.zeros((LANES - states, LANES), f32)], axis=0)
    ends[i] = packed.T[0:8]

    def end_copy(origin, target, sem):
        return remote(ends.at[origin], ends.at[origin], sem, end_recv.at[origin], y, target)

    for k in range(layers - 1, -1, -1):
        for d in range(group):
            if k + d > 0:
                target = sources[k] * group + lax.rem(l + d, group)
                end_copy(i, target, end_send.at[target]).start()
    for d in range(1, count):
        origin = lax.rem(i + count - d, count)
        end_copy(origin, origin, end_send.at[origin]).wait_recv()

    entry = jnp.zeros((1, LANES), f32)
    carried = entry
    entries = []
    for j in range(count):
        entries.append(entry)
        carried = jnp.where(j == i, entry, carried)
        entry = ends[j, 0:1] * entry + ends[j, 1:2]
    state = jnp.zeros((1, LANES), f32)
    returned = state
    for j in range(count - 1, -1, -1):
        returned = jnp.where(j == i, state, returned)
        state = ends[j, 0:1] * state + ends[j, 2:3] + ends[j, 3:4] * entries[j]
    both = jnp.concatenate([carried, returned, jnp.zeros((LANES - 2, LANES), f32)], axis=0).T
    out_ref[...] = back + through * both[0:states, 0:1] + prod_back * both[0:states, 1:2]

    edge_sends(lambda copy: copy.wait_send())
    for k in range(1, layers):
        body_copy(z, sources[k]).wait_send()
    mate_copy(c).wait_send()
    for n in range(3):
        x_copy(n, True).wait_send()
    for n in range(2):
        y_copy(n, True).wait_send()
    for n in range(5):
        pass_copy(n, c).wait_send()

    for k in range(1, layers):
        for cam in range(cams):
            part_copy(k, cam, sources[k] * group + l).wait_send()
    part_copy(0, 1 - y, i).wait_send()
    for d in range(1, count):
        target = lax.rem(i + d, count)
        end_copy(i, target, end_send.at[target]).wait_send()


def block_body(cams, count, group):
    layers = count // group

    def run(keypoints, visibility, expand_weight, dilated_tap_weight, join_weight, decay_rates):
        views, joints, length = keypoints.shape
        channels = expand_weight.shape[2]
        rows = dilated_tap_weight.shape[0]
        states = decay_rates.shape[0]
        keys = jnp.transpose(keypoints, (1, 0, 2))
        taps = jnp.transpose(dilated_tap_weight, (1, 0, 2))
        wide = length + LANES
        steps = 0
        base = 1
        while base < length:
            steps += sum(n * base < length for n in range(1, RADIX))
            base *= RADIX
        dma, vmem = (pltpu.SemaphoreType.DMA, pltpu.VMEM)
        f32, bf16 = jnp.float32, jnp.bfloat16
        sems = [3 * layers] * 2 + [layers] * 2 + [0] * 2 + [3, 3, 2, 2, 5, 5] + [cams * layers] * 2 + [count] * 2
        return pl.pallas_call(
            functools.partial(block_kernel, layers),
            out_shape=jax.ShapeDtypeStruct(decay_rates.shape, f32),
            in_specs=[pl.BlockSpec(memory_space=pl.ANY)] * 6,
            out_specs=pl.BlockSpec(memory_space=pltpu.VMEM),
            scratch_shapes=[
                vmem(keys.shape, jnp.int32),
                vmem(visibility.shape, jnp.int32),
                vmem(expand_weight.shape, bf16),
                vmem((states * cams, channels), bf16),
                vmem(decay_rates.shape, f32),
                dma((6,)),
                vmem((DEPTH, length), f32),
                vmem((layers, DEPTH, length), bf16),
                vmem((16, LANES), bf16),
                vmem((3, layers, 16, LANES), bf16),
                vmem((LANES, LANES), f32),
                vmem((2, LANES, LANES), f32),
                vmem((2 * LANES, channels), f32),
                vmem((views, channels, 3 * DEPTH), bf16),
                vmem((2, 3, 2 * rows, channels), bf16),
                vmem((layers, views, channels, length), bf16),
                vmem((2, channels, views * LANES), bf16),
                vmem((2, 2, 6 * rows, views * LANES), f32),
                vmem((layers, views, 4 * rows, length), bf16),
                vmem((layers, 8, length), f32),
                vmem((cams * states, 4 * rows), bf16),
                vmem((2 * steps, states, length), f32),
                vmem((5, states, length), f32),
                vmem((layers, cams, states, length), bf16),
                vmem((cams * layers, states, length), bf16),
                vmem((count, 8, LANES), f32),
            ]
            + [dma((n,)) if n else dma for n in sems],
            compiler_params=pltpu.CompilerParams(
                collective_id=0, has_side_effects=True, vmem_limit_bytes=58 * 1024 * 1024
            ),
        )(keys, visibility, expand_weight, taps, join_weight.T, decay_rates)

    return run


def solution(mesh):
    cams, count = mesh.shape["cam"], mesh.shape["tm"]
    group = 4
    fits = count % group == 0 and cams == 2 and count == 4 * group
    return jax.shard_map(
        block_body(cams, count, group) if fits else body,
        mesh=mesh,
        in_specs=(
            P("cam", None, "tm"),
            P(None, "tm"),
            P(),
            P("tm", None, None),
            P(),
            P("cam", "tm"),
        ),
        out_specs=P("cam", "tm"),
        check_vma=False,
    )
```
